32 devices in a mesh: seq: 8 (over z, x), dp: 4 (over y, core).
Axes of the slice: x: 2, y: 2, z: 4, core: 2. Of those that a mesh axis runs over, the one named last changes fastest.
Arguments:
- features: bfloat16 [4, 2048, 2048], P('dp', 'seq'), may hold values from -6 to 6
- key_proj: bfloat16 [4, 2048, 128], P('dp', 'seq'), may hold values from -6 to 6
- query_proj: bfloat16 [4, 2048, 128], P('dp', 'seq'), may hold values from -6 to 6
- log_decay: float32 [4, 32, 2048], P('dp', None, 'seq'), may hold values from -0.002 to 0
- doc_start: int32 [4, 2048], P('dp', 'seq'), may hold values from 0 to 1, as said below
- loss_weight: float32 [4, 2048], P('dp', 'seq'), may hold values from 0.25 to 6
- target: bfloat16 [4, 2048, 2048], P('dp', 'seq'), may hold values from -6 to 6
Outputs:
- outputs: bfloat16 [4, 2048, 2048], P('dp', 'seq')
- grad_features: bfloat16 [4, 2048, 2048], P('dp', 'seq')
- grad_keys: bfloat16 [4, 2048, 128], P('dp', 'seq')
- grad_queries: bfloat16 [4, 2048, 128], P('dp', 'seq')
- grad_decay: float32 [4, 32, 2048], P('dp', None, 'seq')
The draws below stay inside these ranges and needn't reach their ends.
Inputs may be any that keep to these rules, and one draw needn't show every extreme that they name: `doc_start`: position 0 of every row begins a document; a document runs from its 1 to the next 1 or the row's end and holds at most 1024 tokens; every row holds one of exactly 1024.
All inputs are finite; a program needn't handle non-finite values.
Results may differ from the reference program's by a relative error of at most 0.0085.
Values sent between devices are 32-bit elements; how exact they have to be, the bound alone decides.
A program may use at most 64 MiB of HBM per device.

```python
import math
import jax
import jax.numpy as jnp
from jax import lax

H = 32
P_SIZE = 64
N = 128
BLOCK = 256
TOK_SEQ = 256
ROWS = 4
SEQ_LEN = 2048
DOC_MOST = 1024


def draw_log_decay(key, part):
    key_rate, key_rough, key_block = jax.random.split(key, 3)
    low_end = math.log(2e-05)
    high_end = math.log(0.001)
    head_rate = jnp.exp(jax.random.uniform(key_rate, (ROWS, H, 1), jnp.float32, low_end, high_end))
    roughness = jax.random.uniform(key_rough, (ROWS, H, SEQ_LEN), jnp.float32, 1.0, 2.0)
    shards = SEQ_LEN // TOK_SEQ
    block_scale = jax.random.uniform(key_block, (ROWS, H, shards, 1), jnp.float32, 0.5, 1.0)
    block_scale = jnp.broadcast_to(block_scale, (ROWS, H, shards, TOK_SEQ)).reshape(ROWS, H, SEQ_LEN)
    return -head_rate * roughness * block_scale


def draw_doc_start(key, part):
    row_keys = jax.random.split(key, ROWS)

    def one_row(row_key):
        key_len, key_pick = jax.random.split(row_key)
        lengths = jax.random.randint(key_len, (SEQ_LEN,), 1, DOC_MOST + 1)
        chosen = jax.random.randint(key_pick, (), 0, 2)
        lengths = jnp.where(jnp.arange(SEQ_LEN) == chosen, DOC_MOST, lengths)
        offsets = jnp.cumsum(lengths) - lengths
        return jnp.zeros((SEQ_LEN,), jnp.int32).at[offsets].set(1, mode='drop')
    return jax.vmap(one_row)(row_keys)


def draw_loss_weight(key, part):
    position = jnp.arange(SEQ_LEN, dtype=jnp.float32)[None, :] / SEQ_LEN
    row_share = jnp.arange(ROWS, dtype=jnp.float32)[:, None] / ROWS
    rising = 1.0 + position + row_share
    base_weight = jax.random.uniform(key, (ROWS, SEQ_LEN), jnp.float32, 0.5, 1.5)
    return base_weight * rising


def steps_of(stream_key, dims, cuts, least, largest):
    loudness = 1.0
    for dim, parts in cuts:
        steps = jax.random.uniform(jax.random.fold_in(jax.random.fold_in(stream_key, 6), dim), (parts,), jnp.float32, least / len(cuts), largest / len(cuts))
        loudness = loudness * jnp.repeat(jnp.exp(steps), dims[dim] // parts).reshape((-1,) + (1,) * (len(dims) - 1 - dim))
    return loudness


def centred(own_key, extent, spread, limit, cuts=(), held_as=jnp.bfloat16):
    result = spread * jax.random.normal(own_key, extent, jnp.float32)
    if cuts:
        result = result * steps_of(own_key, extent, cuts, -0.22, 0.18)
    return jnp.clip(result, -limit, limit).astype(held_as)


def setup_inputs(seed: int = 0) -> dict:
    key_of = jax.random.split(jax.random.key(seed), 8)
    features = centred(key_of[0], (ROWS, SEQ_LEN, H * P_SIZE), 1.0, 6.0, ((0, 4), (1, 8)))
    key_proj = centred(key_of[1], (ROWS, SEQ_LEN, N), 1.0, 6.0, ((0, 4), (1, 8)))
    query_proj = centred(key_of[2], (ROWS, SEQ_LEN, N), 1.0, 6.0, ((0, 4), (1, 8)))
    log_decay = draw_log_decay(jax.random.fold_in(key_of[7], 71), 0)
    doc_start = draw_doc_start(jax.random.fold_in(key_of[7], 71), 0)
    loss_weight = draw_loss_weight(jax.random.fold_in(key_of[7], 71), 0)
    target = centred(key_of[6], (ROWS, SEQ_LEN, H * P_SIZE), 1.0, 6.0, ((0, 4), (1, 8)))
    return dict(features=features, key_proj=key_proj, query_proj=query_proj, log_decay=log_decay, doc_start=doc_start, loss_weight=loss_weight, target=target)


exact_mode = lax.Precision.HIGHEST

def block_tail(values, key_rows, running, segment):
    last_segment = segment[-1]
    tail_weight = jnp.where(segment[None, :] == last_segment, jnp.exp(running[:, -1:] - running), 0.0)
    fresh = jnp.einsum('sn,shp->hpn', key_rows, values * tail_weight.T[:, :, None], precision=exact_mode)
    keep_gain = jnp.exp(running[:, -1]) * (last_segment == 0).astype(jnp.float32)
    return (fresh, keep_gain)

def unpack(feature, key_in, decay_log, starts, key_scale):
    heads = decay_log.shape[0]
    length = feature.shape[0]
    values = feature.astype(jnp.float32).reshape(length, heads, feature.shape[1] // heads)
    key_rows = key_in.astype(jnp.float32) * key_scale
    running = jnp.cumsum(decay_log, axis=1)
    segment = jnp.cumsum(starts)
    return (values, key_rows, running, segment)

def block_step(carry_state, block_piece, key_scale):
    feature, key_in, query_in, decay_log, starts = block_piece
    values, key_rows, running, segment = unpack(feature, key_in, decay_log, starts, key_scale)
    query_rows = query_in.astype(jnp.float32)
    length = values.shape[0]
    position = jnp.arange(length)
    linked = (position[:, None] >= position[None, :]) & (segment[:, None] == segment[None, :])
    scores = jnp.dot(query_in, key_in.T, preferred_element_type=jnp.float32) * key_scale
    mixing = jnp.where(linked, scores, 0.0).astype(jnp.bfloat16)
    mixing = lax.optimization_barrier(mixing)
    lifted = (values * jnp.exp(-running).T[:, :, None]).astype(jnp.bfloat16).reshape(length, -1)
    lifted = lax.optimization_barrier(lifted)
    rise = jnp.exp(running).T
    inner_part = jnp.dot(mixing, lifted, preferred_element_type=jnp.float32).reshape(values.shape) * rise[:, :, None]
    opened = (segment == 0).astype(jnp.float32)
    entry_gain = rise * opened[:, None]
    carried = jnp.einsum('tn,hpn->thp', query_rows, carry_state, precision=exact_mode) * entry_gain[:, :, None]
    fresh, keep_gain = block_tail(values, key_rows, running, segment)
    new_state = keep_gain[:, None, None] * carry_state + fresh
    return (new_state, (inner_part + carried).reshape(length, -1))

def split_blocks(feature, key_in, query_in, decay_log, starts):
    blocks = feature.shape[0] // BLOCK
    heads = decay_log.shape[0]
    return (feature.reshape(blocks, BLOCK, feature.shape[1]), key_in.reshape(blocks, BLOCK, key_in.shape[1]), query_in.reshape(blocks, BLOCK, query_in.shape[1]), decay_log.reshape(heads, blocks, BLOCK).transpose(1, 0, 2), starts.reshape(blocks, BLOCK))

def process(feature, key_in, query_in, decay_log, starts, carry_state):
    key_scale = 1.0 / math.sqrt(key_in.shape[1] * BLOCK)
    pieces = split_blocks(feature, key_in, query_in, decay_log, starts)

    def advance(current, block_piece):
        return block_step(current, block_piece, key_scale)
    final_state, results = lax.scan(advance, carry_state, pieces)
    return (results.reshape(feature.shape[0], feature.shape[1]), final_state)

def reference(features, key_proj, query_proj, log_decay, doc_start, loss_weight, target):
    mean_weight = jnp.mean(loss_weight)

    def one_row(row_pieces):
        feature, key_in, query_in, decay_log, starts, weight, target_row = row_pieces
        empty_state = jnp.zeros((H, P_SIZE, N), jnp.float32)

        def forward(first, second, third, fourth):
            return process(first, second, third, fourth, starts, empty_state)[0]
        output, pullback = jax.vjp(forward, feature, key_in, query_in, decay_log)
        grad_out = (weight / mean_weight)[:, None] * (output - target_row.astype(jnp.float32))
        gradients = pullback(grad_out)
        return (output.astype(jnp.bfloat16), gradients[0], gradients[1], gradients[2], gradients[3])
    results = lax.map(one_row, (features, key_proj, query_proj, log_decay, doc_start, loss_weight, target))
    return (results[0], results[1], results[2], results[3], results[4])
```

```python
import functools
import math

import jax
import jax.numpy as jnp
from jax import lax
from jax.experimental import pallas as pl
from jax.experimental.pallas import tpu as pltpu
from jax.sharding import PartitionSpec as P

F32 = jnp.float32
BF16 = jnp.bfloat16
MESH = pl.DeviceIdType.MESH
CHUNK = 128
EARLY = 3
MIDDLE = 7
SUM_AT = 4
LAG_LAST = 3
LAG_CAP = 16
LAG_PAIR = 5
RELAY_F = (0, 0, 0)
RELAY_B = (0, 0, 0)


def mm(a, b):
    return jnp.dot(a, b, preferred_element_type=F32)


def mm_nt(a, b):
    return lax.dot_general(a, b, (((1,), (1,)), ((), ())), preferred_element_type=F32)


def split(x):
    hi = x.astype(BF16)
    lo = (x - hi.astype(F32)).astype(BF16)
    return hi, lo


def kernel(
    n_seq, n_dp, heads,
    f_hbm, k_hbm, q_hbm, ld_hbm, ds_hbm, w_hbm, t_hbm,
    out_ref, gf_ref, gk_ref, gq_ref, gd_ref,
    xf_send, xf_recv, zf_send, zf_recv, xb_send, xb_recv, zb_send, zb_recv, g_send, g_recv,
    rise_s, inv_s, y_s, dl_s, lift_s, so_s,
    dmix_s, dmixt_s, dq_s, dk_s, gk_s, rt_s, ex_s,
    wown, wdp, wrow, wside, wpair, wup, wdown, wlow, whigh, om_s,
    f_ref, k_ref, q_ref, ld_ref, ds_ref, w_ref, t_ref, in_sem,
    xfs, xfr, zfs, zfr, xbs, xbr, zbs, zbr, rfs, rbs, wds, wdr, ones, oner,
):
    length, width = f_ref.shape
    state = k_ref.shape[1]
    head_size = width // heads
    chunks = width // CHUNK
    per_chunk = CHUNK // head_size
    sigma = 1.0 / math.sqrt(state * length)

    me = lax.axis_index("seq")
    row = lax.axis_index("dp")
    pair = me // 2
    pairs = n_seq // 2
    is_odd = me % 2
    odd = is_odd == 1
    partner = me + 1 - 2 * is_odd

    fetches = [
        pltpu.make_async_copy(src, dst, in_sem.at[i])
        for i, (src, dst) in enumerate(
            [
                (ld_hbm, ld_ref), (ds_hbm, ds_ref), (w_hbm, w_ref), (k_hbm, k_ref),
                (q_hbm, q_ref), (f_hbm, f_ref), (t_hbm, t_ref),
            ]
        )
    ]
    for fetch in fetches:
        fetch.start()
    barrier = pltpu.get_barrier_semaphore()

    def greet(target):
        pl.semaphore_signal(barrier, inc=1, device_id=target, device_id_type=MESH)

    def greet_dp(d, _):
        greet({"dp": (row + d) % n_dp})
        return 0

    has_low = pair > 0
    has_high = pair < pairs - 1
    greet({"seq": partner})

    @pl.when(has_low)
    def _():
        greet({"seq": me - 2})

    @pl.when(has_high)
    def _():
        greet({"seq": me + 2})

    lax.fori_loop(1, n_dp, greet_dp, 0)
    greeters = n_dp + has_low.astype(jnp.int32) + has_high.astype(jnp.int32)

    for fetch in fetches[:5]:
        fetch.wait()
    wown[...] = jnp.broadcast_to(jnp.sum(w_ref[...], axis=1, keepdims=True), wown.shape)

    starts = ds_ref[...].astype(F32)
    table = jnp.concatenate(
        [
            ld_ref[...],
            jnp.broadcast_to(starts, (8, length)),
            jnp.broadcast_to(w_ref[...], (8, length)),
            jnp.zeros((128 - heads - 16, length), F32),
        ],
        axis=0,
    )
    rows_i = lax.broadcasted_iota(jnp.int32, (length, length), 0)
    cols_i = lax.broadcasted_iota(jnp.int32, (length, length), 1)
    lower = (rows_i >= cols_i).astype(F32).astype(BF16)
    upper = (rows_i <= cols_i).astype(F32).astype(BF16)
    eye = (rows_i == cols_i).astype(F32).astype(BF16)
    eye_n = eye[:state, :state]
    table_hi, table_lo = split(table)
    cumulative = mm_nt(lower, table_hi) + mm_nt(lower, table_lo)
    turned = mm_nt(eye, table_hi) + mm_nt(eye, table_lo)
    seg_col = cumulative[:, heads:heads + 1]
    seg_row = mm(jnp.broadcast_to(starts, (8, length)).astype(BF16), upper)[0:1]
    last_seg = jnp.sum(starts, axis=1, keepdims=True)
    tail_row = (seg_row == last_seg).astype(F32)
    tail_col = (seg_col == last_seg).astype(F32)
    open_row = (seg_row == 0.0).astype(F32)
    open_col = (seg_col == 0.0).astype(F32)
    whole_block = (last_seg == 0.0).astype(F32)
    run_hi, run_lo = split(cumulative)

    keys = k_ref[...]
    queries = q_ref[...]
    keys_t = (mm_nt(eye_n, keys) * tail_row).astype(BF16)
    queries_t = (mm_nt(eye_n, queries) * open_row).astype(BF16)
    keys_tail = (keys.astype(F32) * tail_col).astype(BF16)
    queries_open = (queries.astype(F32) * open_col).astype(BF16)

    head_i = lax.broadcasted_iota(jnp.int32, (128, CHUNK), 0)
    lane_h = lax.broadcasted_iota(jnp.int32, (128, CHUNK), 1) // head_size

    def spread(c):
        return (head_i == lane_h + c * per_chunk).astype(F32).astype(BF16)

    def lanes(c):
        return pl.ds(pl.multiple_of(c * CHUNK, CHUNK), CHUNK)

    def to_partner(send, recv, ss, rs, c):
        return pltpu.make_async_remote_copy(
            src_ref=send.at[c], dst_ref=recv.at[c], send_sem=ss.at[c], recv_sem=rs.at[c],
            device_id={"seq": partner}, device_id_type=MESH,
        )

    def to_pair(send, recv, ss, rs, c, target):
        return pltpu.make_async_remote_copy(
            src_ref=send.at[c], dst_ref=recv.at[c], send_sem=ss.at[c], recv_sem=rs.at[c],
            device_id={"seq": target}, device_id_type=MESH,
        )

    def single(src, dst, i, target):
        return pltpu.make_async_remote_copy(
            src_ref=src, dst_ref=dst, send_sem=ones.at[i], recv_sem=oner.at[i],
            device_id={"seq": target}, device_id_type=MESH,
        )

    def relayed(table, at, generic):
        if len(table) != pairs - 1:
            return generic
        count = jnp.int32(0)
        for i, n in enumerate(table):
            count = jnp.where(at == i, n * chunks // 16, count)
        return count

    relay_f_in = jnp.where(has_low, relayed(RELAY_F, pair - 1, 0), 0)
    relay_f_out = jnp.where(has_high, relayed(RELAY_F, pair, 0), 0)
    relay_b_in = jnp.where(has_high, relayed(RELAY_B, pair, 0), 0)
    relay_b_out = jnp.where(has_low, relayed(RELAY_B, pair - 1, 0), 0)
    even = is_odd == 0

    def is_relayed_f(c):
        return odd & (c >= chunks - relay_f_in)

    def crosses_f(c):
        return has_high & (c < chunks - relay_f_out)

    def is_relayed_b(c):
        return even & (c < relay_b_in)

    def crosses_b(c):
        return has_low & (c >= relay_b_out)

    def relay_f(c):
        return to_partner(zf_recv, zf_recv, rfs, zfr, c)

    def relay_b(c):
        return to_partner(zb_recv, zb_recv, rbs, zbr, c)

    def w_dp(d):
        return pltpu.make_async_remote_copy(
            src_ref=wrow, dst_ref=wdp.at[d - 1], send_sem=wds.at[d - 1], recv_sem=wdr.at[d - 1],
            device_id={"dp": (row + d) % n_dp}, device_id_type=MESH,
        )

    chunk_i = lax.broadcasted_iota(jnp.int32, (chunks, 128), 0)
    of_chunk = lax.broadcasted_iota(jnp.int32, (chunks, 128), 1) // per_chunk
    of_lane = (head_i % per_chunk == lane_h).astype(F32).astype(BF16)

    def pick(part):
        last = jnp.broadcast_to(part[length - 1:length].astype(F32), (chunks, 128))
        return mm(jnp.where(of_chunk == chunk_i, last, 0.0).astype(BF16), of_lane)

    g_send[...] = jnp.exp(pick(run_hi) + pick(run_lo)) * whole_block

    def fresh_step(c, _):
        e = spread(c)
        run_x = mm(run_hi, e) + mm(run_lo, e)
        rise = jnp.exp(run_x)
        inv = jnp.exp(-run_x)
        lifted = (f_ref[:, lanes(c)].astype(F32) * inv).astype(BF16)
        xf_send[c] = mm(keys_t, lifted) * (rise[length - 1:length] * sigma)
        rise_s[c] = rise
        inv_s[c] = inv
        lift_s[c] = lifted
        return 0

    def send_fresh(c, _):
        @pl.when(even | crosses_f(c))
        def _():
            to_partner(xf_send, xf_recv, xfs, xfr, c).start()

        return 0

    def fresh_and_send(c, _):
        fresh_step(c, 0)
        send_fresh(c, 0)
        return 0

    def start_w(d, _):
        w_dp(d).start()
        return 0

    fetches[5].wait()
    first = min(EARLY, chunks)
    lax.fori_loop(0, first, fresh_step, 0)
    pl.semaphore_wait(barrier, greeters)
    single(g_send, g_recv, 0, partner).start()
    single(wown, wside, 1, partner).start()
    lax.fori_loop(0, first, send_fresh, 0)
    middle = min(MIDDLE, chunks)
    lax.fori_loop(first, middle, fresh_and_send, 0)
    single(wown, wside, 1, partner).wait_recv()
    wrow[...] = wown[...] + wside[...]
    lax.fori_loop(1, n_dp, start_w, 0)
    lax.fori_loop(middle, chunks, fresh_and_send, 0)

    def add_w(d, total):
        w_dp(d).wait_recv()
        return total + wdp[d - 1]

    linked = (rows_i >= cols_i) & (seg_col == seg_row)
    linked_t = (rows_i <= cols_i) & (seg_col == seg_row)
    mixing = jnp.where(linked, mm_nt(queries, keys) * sigma, 0.0).astype(BF16)
    mixing_t = jnp.where(linked_t, mm_nt(keys, queries) * sigma, 0.0).astype(BF16)

    @pl.when(pair == 0)
    def _():
        zf_recv[...] = jnp.zeros_like(zf_recv)
        wlow[...] = jnp.zeros_like(wlow)

    @pl.when(pair == pairs - 1)
    def _():
        zb_recv[...] = jnp.zeros_like(zb_recv)
        whigh[...] = jnp.zeros_like(whigh)

    dmix_s[...] = jnp.zeros_like(dmix_s)
    dmixt_s[...] = jnp.zeros_like(dmixt_s)
    dq_s[...] = jnp.zeros_like(dq_s)
    dk_s[...] = jnp.zeros_like(dk_s)
    rt_s[...] = jnp.zeros_like(rt_s)
    ex_s[...] = jnp.zeros_like(ex_s)

    def inner_step(c, _):
        y_s[c] = mm(mixing, lift_s[c])
        return 0

    lax.fori_loop(0, chunks, inner_step, 0)

    single(g_send, g_recv, 0, partner).wait_recv()
    fetches[6].wait()
    weight = turned[:, heads + 8:heads + 9]

    def forward_step(c, _):
        @pl.when(has_low)
        def _():
            to_pair(zf_send, zf_recv, zfs, zfr, c, me).wait_recv()

        @pl.when(is_relayed_f(c))
        def _():
            relay_f(c).start()

        @pl.when(odd | crosses_f(c))
        def _():
            to_partner(xf_send, xf_recv, xfs, xfr, c).wait_recv()

        @pl.when(c == min(SUM_AT, chunks - 1))
        def _():
            wpair[...] = lax.fori_loop(1, n_dp, add_w, wrow[...])

            @pl.when(has_low)
            def _():
                single(wup, wlow, 2, me).wait_recv()

            wup[...] = wlow[...] + wpair[...]

            @pl.when(has_high)
            def _():
                single(wup, wlow, 2, me + 2).start()

        own = xf_send[c]
        own_keep = g_send[pl.ds(c, 1), :]
        other = xf_recv[c]
        other_keep = g_recv[pl.ds(c, 1), :]
        entry = zf_recv[c]
        before = jnp.where(odd, other + other_keep * entry, entry)
        after = own + own_keep * before
        zf_send[c] = jnp.where(odd, after, other + other_keep * after)

        @pl.when((odd & has_high) | crosses_f(c))
        def _():
            to_pair(zf_send, zf_recv, zfs, zfr, c, me + 2).start()

        so_s[c] = after
        before_h = before.astype(BF16)
        rise = rise_s[c]
        y = rise * (y_s[c] + mm(queries_open, before_h))
        out_ref[:, lanes(c)] = y.astype(BF16)
        grad = weight * (y - t_ref[:, lanes(c)].astype(F32))
        z = (grad * rise).astype(BF16)
        xb_send[c] = mm(queries_t, z)

        @pl.when(odd | crosses_b(c))
        def _():
            to_partner(xb_send, xb_recv, xbs, xbr, c).start()

        y_s[c] = grad * y
        dq_s[...] += mm_nt(z, before_h)
        lifted = lift_s[c]
        dmix_s[...] += mm_nt(z, lifted)
        dmixt_s[...] += mm_nt(lifted, z)
        dl_s[c] = mm(mixing_t, z)
        return 0

    def backward_step(c, _):
        @pl.when(has_high)
        def _():
            to_pair(zb_send, zb_recv, zbs, zbr, c, me).wait_recv()

        @pl.when(is_relayed_b(c))
        def _():
            relay_b(c).start()

        @pl.when(even | crosses_b(c))
        def _():
            to_partner(xb_send, xb_recv, xbs, xbr, c).wait_recv()

        @pl.when(c == 0)
        def _():
            @pl.when(has_high)
            def _():
                single(wdown, whigh, 3, me).wait_recv()

            pair_sum = wpair[...]
            wdown[...] = whigh[...] + pair_sum

            @pl.when(has_low)
            def _():
                single(wdown, whigh, 3, me - 2).start()

            om_s[...] = (length * n_seq * n_dp) / (wlow[...] + pair_sum + whigh[...])

        own = xb_send[c]
        own_keep = g_send[pl.ds(c, 1), :]
        other = xb_recv[c]
        other_keep = g_recv[pl.ds(c, 1), :]
        entry = zb_recv[c]
        adjoint = jnp.where(odd, entry, other + other_keep * entry)
        onward = own + own_keep * adjoint
        zb_send[c] = jnp.where(odd, other + other_keep * onward, onward)

        @pl.when((even & has_low) | crosses_b(c))
        def _():
            to_pair(zb_send, zb_recv, zbs, zbr, c, me - 2).start()

        over_mean = om_s[0:1, 0:1]

        e = spread(c)
        gain = rise_s[c, length - 1:length, :]
        adjoint = adjoint * over_mean
        scaled = (adjoint * (gain * sigma)).astype(BF16)
        d_feature = inv_s[c] * (dl_s[c] * over_mean + mm(keys_tail, scaled))
        gf_ref[:, lanes(c)] = d_feature.astype(BF16)
        change = y_s[c] * over_mean - f_ref[:, lanes(c)].astype(F32) * d_feature
        change_hi, change_lo = split(change)
        rt_s[...] += mm_nt(e, change_hi) + mm_nt(e, change_lo)
        dk_s[...] += mm_nt(lift_s[c], scaled)
        end_hi, end_lo = split(adjoint * so_s[c])
        ex_s[...] += mm_nt(e, end_hi) + mm_nt(e, end_lo)
        return 0

    def finish_scores():
        over_mean = om_s[0:1, 0:1]
        d_scores = (jnp.where(linked, dmix_s[...], 0.0) * (over_mean * sigma)).astype(BF16)
        d_scores_t = (jnp.where(linked_t, dmixt_s[...], 0.0) * (over_mean * sigma)).astype(BF16)
        gq_ref[...] = (mm(d_scores, keys) + (open_col * over_mean) * dq_s[...]).astype(BF16)
        gk_s[...] = mm(d_scores_t, queries)

    lag = jnp.minimum(
        LAG_CAP * chunks // 16,
        jnp.maximum(min(SUM_AT, chunks - 1), LAG_LAST + LAG_PAIR * (pairs - 1 - pair)),
    )

    def step(i, _):
        @pl.when(i < chunks)
        def _():
            forward_step(i, 0)

        @pl.when((i >= lag) & (i < lag + chunks))
        def _():
            backward_step(i - lag, 0)

        @pl.when(i == jnp.maximum(chunks, lag + 1))
        def _():
            finish_scores()

        return 0

    lax.fori_loop(0, chunks + jnp.maximum(lag, 2), step, 0)

    gk_ref[...] = (gk_s[...] + tail_col * dk_s[...]).astype(BF16)
    rt_hi, rt_lo = split(rt_s[...])
    decay = mm(rt_hi, lower) + mm(rt_lo, lower) + jnp.sum(ex_s[...], axis=1, keepdims=True)
    gd_ref[...] = decay[:heads]

    def finish_step(c, _):
        @pl.when(even | crosses_f(c))
        def _():
            to_partner(xf_send, xf_recv, xfs, xfr, c).wait_send()

        @pl.when(odd | crosses_b(c))
        def _():
            to_partner(xb_send, xb_recv, xbs, xbr, c).wait_send()

        @pl.when((odd & has_high) | crosses_f(c))
        def _():
            to_pair(zf_send, zf_recv, zfs, zfr, c, me + 2).wait_send()

        @pl.when((even & has_low) | crosses_b(c))
        def _():
            to_pair(zb_send, zb_recv, zbs, zbr, c, me - 2).wait_send()

        @pl.when(is_relayed_f(c))
        def _():
            relay_f(c).wait_send()

        @pl.when(is_relayed_b(c))
        def _():
            relay_b(c).wait_send()

        return 0

    lax.fori_loop(0, chunks, finish_step, 0)

    def finish_w(d, _):
        w_dp(d).wait_send()
        return 0

    lax.fori_loop(1, n_dp, finish_w, 0)
    single(g_send, g_recv, 0, partner).wait_send()
    single(wown, wside, 1, partner).wait_send()

    @pl.when(has_high)
    def _():
        single(wup, wlow, 2, me + 2).wait_send()

    @pl.when(has_low)
    def _():
        single(wdown, whigh, 3, me - 2).wait_send()


def store_kernel(*refs):
    count = len(refs) // 2
    sem = refs[-1]
    copies = [
        pltpu.make_async_copy(refs[i], refs[count + i], sem.at[i]) for i in range(count)
    ]
    for copy in copies:
        copy.start()
    for copy in copies:
        copy.wait()


def body(features, key_proj, query_proj, log_decay, doc_start, loss_weight, target):
    n_seq, n_dp = lax.axis_size("seq"), lax.axis_size("dp")
    length, width = features.shape[1:]
    state = key_proj.shape[2]
    heads = log_decay.shape[1]
    chunks = width // CHUNK
    vmem = pl.BlockSpec(memory_space=pltpu.VMEM)
    big = (chunks, length, CHUNK)
    small = (chunks, state, CHUNK)
    scratch = [
        pltpu.VMEM(small, F32), pltpu.VMEM(small, F32),
        pltpu.VMEM(small, F32), pltpu.VMEM(small, F32),
        pltpu.VMEM(small, F32), pltpu.VMEM(small, F32),
        pltpu.VMEM(small, F32), pltpu.VMEM(small, F32),
        pltpu.VMEM((chunks, CHUNK), F32), pltpu.VMEM((chunks, CHUNK), F32),
        pltpu.VMEM(big, F32), pltpu.VMEM(big, F32), pltpu.VMEM(big, F32), pltpu.VMEM(big, F32),
        pltpu.VMEM(big, BF16), pltpu.VMEM(small, F32),
        pltpu.VMEM((length, length), F32), pltpu.VMEM((length, length), F32),
        pltpu.VMEM((length, state), F32), pltpu.VMEM((length, state), F32),
        pltpu.VMEM((length, state), F32), pltpu.VMEM((128, length), F32), pltpu.VMEM((128, state), F32),
        pltpu.VMEM((8, 128), F32), pltpu.VMEM((n_dp - 1, 8, 128), F32),
    ]
    scratch += [pltpu.VMEM((8, 128), F32)] * 8
    scratch += [
        pltpu.VMEM((length, width), BF16), pltpu.VMEM((length, state), BF16),
        pltpu.VMEM((length, state), BF16), pltpu.VMEM((heads, length), F32),
        pltpu.VMEM((1, length), jnp.int32), pltpu.VMEM((1, length), F32),
        pltpu.VMEM((length, width), BF16), pltpu.SemaphoreType.DMA((7,)),
    ]
    scratch += [pltpu.SemaphoreType.DMA((chunks,))] * 10
    scratch += [pltpu.SemaphoreType.DMA((n_dp - 1,))] * 2
    scratch += [pltpu.SemaphoreType.DMA((4,))] * 2
    shapes = (
        ((length, width), BF16),
        ((length, width), BF16),
        ((length, state), BF16),
        ((length, state), BF16),
        ((heads, length), F32),
    )
    results = pl.pallas_call(
        functools.partial(kernel, n_seq, n_dp, heads),
        out_shape=tuple(pltpu.VMEM(*shape) for shape in shapes),
        in_specs=[pl.BlockSpec(memory_space=pltpu.HBM)] * 7,
        out_specs=(vmem,) * 5,
        scratch_shapes=scratch,
        compiler_params=pltpu.CompilerParams(
            collective_id=0, has_side_effects=True, vmem_limit_bytes=44 << 20
        ),
        name="mixing",
    )(
        *(
            pltpu.with_memory_space_constraint(x, pltpu.HBM)
            for x in (
                features[0], key_proj[0], query_proj[0], log_decay[0], doc_start, loss_weight,
                target[0],
            )
        )
    )
    stored = pl.pallas_call(
        store_kernel,
        out_shape=tuple(jax.ShapeDtypeStruct(*shape) for shape in shapes),
        in_specs=(vmem,) * 5,
        out_specs=(pl.BlockSpec(memory_space=pl.ANY),) * 5,
        scratch_shapes=[pltpu.SemaphoreType.DMA((5,))],
        name="store",
    )(*(pltpu.with_memory_space_constraint(r, pltpu.VMEM) for r in results))
    return tuple(r[None] for r in stored)


def solution(mesh):
    placed = (
        P("dp", "seq", None),
        P("dp", "seq", None),
        P("dp", "seq", None),
        P("dp", None, "seq"),
        P("dp", "seq"),
        P("dp", "seq"),
        P("dp", "seq", None),
    )
    return jax.shard_map(
        body,
        mesh=mesh,
        in_specs=placed,
        out_specs=(
            P("dp", "seq", None),
            P("dp", "seq", None),
            P("dp", "seq", None),
            P("dp", "seq", None),
            P("dp", None, "seq"),
        ),
        check_vma=False,
    )
```

```python
import functools
import math

import jax
import jax.numpy as jnp
from jax import lax
from jax.experimental import pallas as pl
from jax.experimental.pallas import tpu as pltpu
from jax.sharding import PartitionSpec as P

F32 = jnp.float32
BF16 = jnp.bfloat16
MESH = pl.DeviceIdType.MESH
CHUNK = 128
EARLY = 3
SUM_AT = 4
BEHIND = 4
LEAD = (9, 8, 10, 15)
LAG_Y = (10, 11, 6, 7)
LAG_Z = (25, 25, 18, 18)
LAG_B = (30, 34, 31, 32)


def mm(a, b):
    return jnp.dot(a, b, preferred_element_type=F32)


def mm_nt(a, b):
    return lax.dot_general(a, b, (((1,), (1,)), ((), ())), preferred_element_type=F32)


def split(x):
    hi = x.astype(BF16)
    lo = (x - hi.astype(F32)).astype(BF16)
    return hi, lo


def kernel(
    n_seq, n_dp, heads,
    f_hbm, k_hbm, q_hbm, ld_hbm, ds_hbm, w_hbm, t_hbm,
    out_ref, gf_ref, gk_ref, gq_ref, gd_ref,
    xf_send, xf_recv, zf_send, zf_recv, rf_send, xb_send, xb_recv, zb_send, zb_recv, rb_send,
    before_s, adjoint_s, g_send, g_recv,
    rise_s, inv_s, y_s, dl_s, lift_s,
    dmix_s, dmixt_s, dq_s, dk_s, gk_s, rt_s, ex_s,
    wown, wdp, wrow, wside, wpair, wup, wdown, wlow, whigh, om_s,
    f_ref, k_ref, q_ref, ld_ref, ds_ref, w_ref, t_ref, in_sem,
    xfs, xfr, zfs, zfr, rfs, rfr, xbs, xbr, zbs, zbr, rbs, rbr, wds, wdr, ones, oner,
):
    length, width = f_ref.shape
    state = k_ref.shape[1]
    head_size = width // heads
    chunks = width // CHUNK
    per_chunk = CHUNK // head_size
    sigma = 1.0 / math.sqrt(state * length)

    me = lax.axis_index("seq")
    row = lax.axis_index("dp")
    pair = me // 2
    pairs = n_seq // 2
    is_odd = me % 2
    odd = is_odd == 1
    partner = me + 1 - 2 * is_odd

    fetches = [
        pltpu.make_async_copy(src, dst, in_sem.at[i])
        for i, (src, dst) in enumerate(
            [
                (ld_hbm, ld_ref), (ds_hbm, ds_ref), (w_hbm, w_ref), (k_hbm, k_ref),
                (q_hbm, q_ref), (f_hbm, f_ref), (t_hbm, t_ref),
            ]
        )
    ]
    for fetch in fetches:
        fetch.start()
    barrier = pltpu.get_barrier_semaphore()

    def greet(target):
        pl.semaphore_signal(barrier, inc=1, device_id=target, device_id_type=MESH)

    def greet_dp(d, _):
        greet({"dp": (row + d) % n_dp})
        return 0

    has_low = pair > 0
    has_high = pair < pairs - 1
    greet({"seq": partner})

    @pl.when(has_low)
    def _():
        greet({"seq": me - 2})

    @pl.when(has_high)
    def _():
        greet({"seq": me + 2})

    even = is_odd == 0
    lax.fori_loop(1, n_dp, greet_dp, 0)
    greeters = n_dp + sum(flag.astype(jnp.int32) for flag in (has_low, has_high))

    for fetch in fetches[:5]:
        fetch.wait()
    wown[...] = jnp.broadcast_to(jnp.sum(w_ref[...], axis=1, keepdims=True), wown.shape)

    starts = ds_ref[...].astype(F32)
    table = jnp.concatenate(
        [
            ld_ref[...],
            jnp.broadcast_to(starts, (8, length)),
            jnp.broadcast_to(w_ref[...], (8, length)),
            jnp.zeros((128 - heads - 16, length), F32),
        ],
        axis=0,
    )
    rows_i = lax.broadcasted_iota(jnp.int32, (length, length), 0)
    cols_i = lax.broadcasted_iota(jnp.int32, (length, length), 1)
    lower = (rows_i >= cols_i).astype(F32).astype(BF16)
    upper = (rows_i <= cols_i).astype(F32).astype(BF16)
    eye = (rows_i == cols_i).astype(F32).astype(BF16)
    eye_n = eye[:state, :state]
    table_hi, table_lo = split(table)
    cumulative = mm_nt(lower, table_hi) + mm_nt(lower, table_lo)
    turned = mm_nt(eye, table_hi) + mm_nt(eye, table_lo)
    seg_col = cumulative[:, heads:heads + 1]
    seg_row = mm(jnp.broadcast_to(starts, (8, length)).astype(BF16), upper)[0:1]
    last_seg = jnp.sum(starts, axis=1, keepdims=True)
    tail_row = (seg_row == last_seg).astype(F32)
    tail_col = (seg_col == last_seg).astype(F32)
    open_row = (seg_row == 0.0).astype(F32)
    open_col = (seg_col == 0.0).astype(F32)
    whole_block = (last_seg == 0.0).astype(F32)
    run_hi, run_lo = split(cumulative)

    keys = k_ref[...]
    queries = q_ref[...]
    keys_t = (mm_nt(eye_n, keys) * tail_row).astype(BF16)
    queries_t = (mm_nt(eye_n, queries) * open_row).astype(BF16)
    keys_tail = (keys.astype(F32) * tail_col).astype(BF16)
    queries_open = (queries.astype(F32) * open_col).astype(BF16)

    head_i = lax.broadcasted_iota(jnp.int32, (128, CHUNK), 0)
    lane_h = lax.broadcasted_iota(jnp.int32, (128, CHUNK), 1) // head_size

    def spread(c):
        return (head_i == lane_h + c * per_chunk).astype(F32).astype(BF16)

    def lanes(c):
        return pl.ds(pl.multiple_of(c * CHUNK, CHUNK), CHUNK)

    part = state // 2
    mine = pl.ds(pl.multiple_of(is_odd * part, part), part)
    theirs = pl.ds(pl.multiple_of((1 - is_odd) * part, part), part)

    def remote(src, dst, ss, rs, c, target):
        return pltpu.make_async_remote_copy(
            src_ref=src, dst_ref=dst, send_sem=ss.at[c], recv_sem=rs.at[c],
            device_id={"seq": target}, device_id_type=MESH,
        )

    def xf(c):
        return remote(xf_send.at[c, theirs], xf_recv.at[c], xfs, xfr, c, partner)

    def xb(c):
        return remote(xb_send.at[c, theirs], xb_recv.at[c], xbs, xbr, c, partner)

    def zf(c):
        return remote(zf_send.at[c], zf_recv.at[c], zfs, zfr, c, me + 2)

    def zb(c):
        return remote(zb_send.at[c], zb_recv.at[c], zbs, zbr, c, me - 2)

    def rf(c):
        return remote(rf_send.at[c], before_s.at[c, mine], rfs, rfr, c, partner)

    def rb(c):
        return remote(rb_send.at[c], adjoint_s.at[c, mine], rbs, rbr, c, partner)

    def single(src, dst, i, target):
        return pltpu.make_async_remote_copy(
            src_ref=src, dst_ref=dst, send_sem=ones.at[i], recv_sem=oner.at[i],
            device_id={"seq": target}, device_id_type=MESH,
        )

    def look_up(table, at, size, generic):
        if len(table) != size:
            return jnp.int32(generic)
        found = jnp.int32(0)
        for i, n in enumerate(table):
            found = jnp.where(at == i, n * chunks // 16, found)
        return found

    to_next = even | has_high
    from_next = odd | has_high
    to_last = odd | has_low
    from_last = even | has_low

    def w_dp(d):
        return pltpu.make_async_remote_copy(
            src_ref=wrow, dst_ref=wdp.at[d - 1], send_sem=wds.at[d - 1], recv_sem=wdr.at[d - 1],
            device_id={"dp": (row + d) % n_dp}, device_id_type=MESH,
        )

    chunk_i = lax.broadcasted_iota(jnp.int32, (chunks, 128), 0)
    of_chunk = lax.broadcasted_iota(jnp.int32, (chunks, 128), 1) // per_chunk
    of_lane = (head_i % per_chunk == lane_h).astype(F32).astype(BF16)

    def pick(part):
        last = jnp.broadcast_to(part[length - 1:length].astype(F32), (chunks, 128))
        return mm(jnp.where(of_chunk == chunk_i, last, 0.0).astype(BF16), of_lane)

    g_send[...] = jnp.exp(pick(run_hi) + pick(run_lo)) * whole_block

    def fresh_step(c, _):
        e = spread(c)
        run_x = mm(run_hi, e) + mm(run_lo, e)
        rise = jnp.exp(run_x)
        inv = jnp.exp(-run_x)
        lifted = (f_ref[:, lanes(c)].astype(F32) * inv).astype(BF16)
        xf_send[c] = mm(keys_t, lifted) * (rise[length - 1:length] * sigma)
        rise_s[c] = rise
        inv_s[c] = inv
        lift_s[c] = lifted
        return 0

    def send_fresh(c, _):
        @pl.when(to_next)
        def _():
            xf(c).start()

        return 0

    def fresh_and_send(c, _):
        fresh_step(c, 0)
        send_fresh(c, 0)
        return 0

    def start_w(d, _):
        w_dp(d).start()
        return 0

    linked = (rows_i >= cols_i) & (seg_col == seg_row)
    linked_t = (rows_i <= cols_i) & (seg_col == seg_row)
    fetches[5].wait()
    first = min(EARLY, chunks)
    lax.fori_loop(0, first, fresh_step, 0)
    mixing = jnp.where(linked, mm_nt(queries, keys) * sigma, 0.0).astype(BF16)
    mixing_t = jnp.where(linked_t, mm_nt(keys, queries) * sigma, 0.0).astype(BF16)
    dmix_s[...] = jnp.zeros_like(dmix_s)
    dmixt_s[...] = jnp.zeros_like(dmixt_s)
    dq_s[...] = jnp.zeros_like(dq_s)
    dk_s[...] = jnp.zeros_like(dk_s)
    rt_s[...] = jnp.zeros_like(rt_s)
    ex_s[...] = jnp.zeros_like(ex_s)

    @pl.when(pair == 0)
    def _():
        zf_recv[...] = jnp.zeros_like(zf_recv)
        wlow[...] = jnp.zeros_like(wlow)

        @pl.when(even)
        def _():
            before_s[...] = jnp.zeros_like(before_s)

    @pl.when(pair == pairs - 1)
    def _():
        zb_recv[...] = jnp.zeros_like(zb_recv)
        whigh[...] = jnp.zeros_like(whigh)

        @pl.when(odd)
        def _():
            adjoint_s[...] = jnp.zeros_like(adjoint_s)

    lead = jnp.maximum(first, look_up(LEAD, pair, pairs, chunks))
    lag_y = look_up(LAG_Y, pair, pairs, 0)
    sum_at = min(SUM_AT, chunks - 1)
    generic_lag = jnp.minimum(chunks, 3 + 5 * (pairs - 1 - pair))
    lag_z = jnp.maximum(look_up(LAG_Z, pair, pairs, generic_lag), jnp.maximum(lag_y, sum_at))
    lag_b = jnp.maximum(look_up(LAG_B, pair, pairs, generic_lag), lag_z)

    pl.semaphore_wait(barrier, greeters)
    single(g_send, g_recv, 0, partner).start()
    single(wown, wside, 1, partner).start()
    lax.fori_loop(0, first, send_fresh, 0)

    lax.fori_loop(first, lead, fresh_and_send, 0)
    single(wown, wside, 1, partner).wait_recv()
    wrow[...] = wown[...] + wside[...]
    lax.fori_loop(1, n_dp, start_w, 0)
    single(g_send, g_recv, 0, partner).wait_recv()

    fetches[6].wait()
    weight = turned[:, heads + 8:heads + 9]

    def add_w(d, total):
        w_dp(d).wait_recv()
        return total + wdp[d - 1]

    def carry_forward(c):
        @pl.when(c == sum_at)
        def _():
            wpair[...] = lax.fori_loop(1, n_dp, add_w, wrow[...])

            @pl.when(has_low)
            def _():
                single(wup, wlow, 2, me).wait_recv()

            wup[...] = wlow[...] + wpair[...]

            @pl.when(has_high)
            def _():
                single(wup, wlow, 2, me + 2).start()

        @pl.when(has_low)
        def _():
            zf(c).wait_recv()

        @pl.when(from_next)
        def _():
            xf(c).wait_recv()

        own_keep = g_send[pl.ds(c, 1), :]
        other_keep = g_recv[pl.ds(c, 1), :]
        own = xf_send[c, mine]
        other = xf_recv[c]
        entry = zf_recv[c]
        middle = jnp.where(odd, other, own) + jnp.where(odd, other_keep, own_keep) * entry
        zf_send[c] = jnp.where(odd, own, other) + jnp.where(odd, own_keep, other_keep) * middle

        @pl.when(has_high)
        def _():
            zf(c).start()

        rf_send[c] = jnp.where(odd, entry, middle)

        @pl.when(from_last)
        def _():
            rf(c).start()

        before_s[c, mine] = jnp.where(odd, middle, entry)

    def forward_step(c):
        @pl.when(to_last)
        def _():
            rf(c).wait_recv()

        before_h = before_s[c].astype(BF16)
        rise = rise_s[c]
        lifted = lift_s[c]
        y = rise * (mm(mixing, lifted) + mm(queries_open, before_h))
        grad = weight * (y - t_ref[:, lanes(c)].astype(F32))
        z = (grad * rise).astype(BF16)
        xb_send[c] = mm(queries_t, z)

        @pl.when(to_last)
        def _():
            xb(c).start()

        out_ref[:, lanes(c)] = y.astype(BF16)
        y_s[c] = grad * y
        dq_s[...] += mm_nt(z, before_h)
        dmix_s[...] += mm_nt(z, lifted)
        dmixt_s[...] += mm_nt(lifted, z)
        dl_s[c] = mm(mixing_t, z)

    def sent_forward(c):
        @pl.when(to_next)
        def _():
            xf(c).wait_send()

        @pl.when(from_last)
        def _():
            rf(c).wait_send()

        @pl.when(has_high)
        def _():
            zf(c).wait_send()

    def sent_backward(c):
        @pl.when(to_last)
        def _():
            xb(c).wait_send()

        @pl.when(from_next)
        def _():
            rb(c).wait_send()

        @pl.when(has_low)
        def _():
            zb(c).wait_send()

    def carry_backward(c):
        @pl.when(has_high)
        def _():
            zb(c).wait_recv()

        @pl.when(from_last)
        def _():
            xb(c).wait_recv()

        own_keep = g_send[pl.ds(c, 1), :]
        other_keep = g_recv[pl.ds(c, 1), :]
        own = xb_send[c, mine]
        other = xb_recv[c]
        entry = zb_recv[c]
        middle = jnp.where(odd, own, other) + jnp.where(odd, own_keep, other_keep) * entry
        zb_send[c] = jnp.where(odd, other, own) + jnp.where(odd, other_keep, own_keep) * middle

        @pl.when(has_low)
        def _():
            zb(c).start()

        rb_send[c] = jnp.where(odd, middle, entry)

        @pl.when(from_next)
        def _():
            rb(c).start()

        adjoint_s[c, mine] = jnp.where(odd, entry, middle)

        @pl.when(c == 0)
        def _():
            @pl.when(has_high)
            def _():
                single(wdown, whigh, 3, me).wait_recv()

            wdown[...] = whigh[...] + wpair[...]

            @pl.when(has_low)
            def _():
                single(wdown, whigh, 3, me - 2).start()

            om_s[...] = (length * n_seq * n_dp) / (wlow[...] + wpair[...] + whigh[...])

    def backward_step(c):
        @pl.when(to_next)
        def _():
            rb(c).wait_recv()

        over_mean = om_s[0:1, 0:1]
        e = spread(c)
        gain = rise_s[c, length - 1:length, :]
        adjoint = adjoint_s[c] * over_mean
        scaled = (adjoint * (gain * sigma)).astype(BF16)
        d_feature = inv_s[c] * (dl_s[c] * over_mean + mm(keys_tail, scaled))
        gf_ref[:, lanes(c)] = d_feature.astype(BF16)
        change = y_s[c] * over_mean - f_ref[:, lanes(c)].astype(F32) * d_feature
        change_hi, change_lo = split(change)
        rt_s[...] += mm_nt(e, change_hi) + mm_nt(e, change_lo)
        dk_s[...] += mm_nt(lift_s[c], scaled)
        after = xf_send[c] + g_send[pl.ds(c, 1), :] * before_s[c]
        end_hi, end_lo = split(adjoint * after)
        ex_s[...] += mm_nt(e, end_hi) + mm_nt(e, end_lo)
        sent_forward(c)

        @pl.when(c >= BEHIND)
        def _():
            sent_backward(c - BEHIND)

    def finish_scores():
        over_mean = om_s[0:1, 0:1]
        d_scores = (jnp.where(linked, dmix_s[...], 0.0) * (over_mean * sigma)).astype(BF16)
        d_scores_t = (jnp.where(linked_t, dmixt_s[...], 0.0) * (over_mean * sigma)).astype(BF16)
        gq_ref[...] = (mm(d_scores, keys) + (open_col * over_mean) * dq_s[...]).astype(BF16)
        gk_s[...] = mm(d_scores_t, queries)

    def step(i, _):
        @pl.when(i + lead < chunks)
        def _():
            fresh_and_send(i + lead, 0)

        @pl.when(i < chunks)
        def _():
            carry_forward(i)

        @pl.when((i >= lag_y) & (i < lag_y + chunks))
        def _():
            forward_step(i - lag_y)

        @pl.when((i >= lag_z) & (i < lag_z + chunks))
        def _():
            carry_backward(i - lag_z)

        @pl.when(i == jnp.maximum(chunks + lag_y, lag_z + 1))
        def _():
            finish_scores()

        @pl.when((i >= lag_b) & (i < lag_b + chunks))
        def _():
            backward_step(i - lag_b)

        return 0

    lax.fori_loop(0, jnp.maximum(chunks + jnp.maximum(lag_b, lag_y + 1), lag_z + 2), step, 0)

    gk_ref[...] = (gk_s[...] + tail_col * dk_s[...]).astype(BF16)
    rt_hi, rt_lo = split(rt_s[...])
    decay = mm(rt_hi, lower) + mm(rt_lo, lower) + jnp.sum(ex_s[...], axis=1, keepdims=True)
    gd_ref[...] = decay[:heads]

    def finish_step(c, _):
        sent_backward(c)
        return 0

    lax.fori_loop(max(chunks - BEHIND, 0), chunks, finish_step, 0)

    def finish_w(d, _):
        w_dp(d).wait_send()
        return 0

    lax.fori_loop(1, n_dp, finish_w, 0)
    single(g_send, g_recv, 0, partner).wait_send()
    single(wown, wside, 1, partner).wait_send()

    @pl.when(has_high)
    def _():
        single(wup, wlow, 2, me + 2).wait_send()

    @pl.when(has_low)
    def _():
        single(wdown, whigh, 3, me - 2).wait_send()


def store_kernel(*refs):
    count = len(refs) // 2
    sem = refs[-1]
    copies = [
        pltpu.make_async_copy(refs[i], refs[count + i], sem.at[i]) for i in range(count)
    ]
    for copy in copies:
        copy.start()
    for copy in copies:
        copy.wait()


def body(features, key_proj, query_proj, log_decay, doc_start, loss_weight, target):
    n_seq, n_dp = lax.axis_size("seq"), lax.axis_size("dp")
    length, width = features.shape[1:]
    state = key_proj.shape[2]
    heads = log_decay.shape[1]
    chunks = width // CHUNK
    vmem = pl.BlockSpec(memory_space=pltpu.VMEM)
    big = (chunks, length, CHUNK)
    small = (chunks, state, CHUNK)
    half = (chunks, state // 2, CHUNK)
    scratch = [
        pltpu.VMEM(small, F32), pltpu.VMEM(half, F32), pltpu.VMEM(half, F32),
        pltpu.VMEM(half, F32), pltpu.VMEM(half, F32),
        pltpu.VMEM(small, F32), pltpu.VMEM(half, F32), pltpu.VMEM(half, F32),
        pltpu.VMEM(half, F32), pltpu.VMEM(half, F32),
        pltpu.VMEM(small, F32), pltpu.VMEM(small, F32),
        pltpu.VMEM((chunks, CHUNK), F32), pltpu.VMEM((chunks, CHUNK), F32),
        pltpu.VMEM(big, F32), pltpu.VMEM(big, F32), pltpu.VMEM(big, F32), pltpu.VMEM(big, F32),
        pltpu.VMEM(big, BF16),
        pltpu.VMEM((length, length), F32), pltpu.VMEM((length, length), F32),
        pltpu.VMEM((length, state), F32), pltpu.VMEM((length, state), F32),
        pltpu.VMEM((length, state), F32), pltpu.VMEM((128, length), F32), pltpu.VMEM((128, state), F32),
        pltpu.VMEM((8, 128), F32), pltpu.VMEM((n_dp - 1, 8, 128), F32),
    ]
    scratch += [pltpu.VMEM((8, 128), F32)] * 8
    scratch += [
        pltpu.VMEM((length, width), BF16), pltpu.VMEM((length, state), BF16),
        pltpu.VMEM((length, state), BF16), pltpu.VMEM((heads, length), F32),
        pltpu.VMEM((1, length), jnp.int32), pltpu.VMEM((1, length), F32),
        pltpu.VMEM((length, width), BF16), pltpu.SemaphoreType.DMA((7,)),
    ]
    scratch += [pltpu.SemaphoreType.DMA((chunks,))] * 12
    scratch += [pltpu.SemaphoreType.DMA((n_dp - 1,))] * 2
    scratch += [pltpu.SemaphoreType.DMA((4,))] * 2
    shapes = (
        ((length, width), BF16),
        ((length, width), BF16),
        ((length, state), BF16),
        ((length, state), BF16),
        ((heads, length), F32),
    )
    results = pl.pallas_call(
        functools.partial(kernel, n_seq, n_dp, heads),
        out_shape=tuple(pltpu.VMEM(*shape) for shape in shapes),
        in_specs=[pl.BlockSpec(memory_space=pltpu.HBM)] * 7,
        out_specs=(vmem,) * 5,
        scratch_shapes=scratch,
        compiler_params=pltpu.CompilerParams(
            collective_id=0, has_side_effects=True, vmem_limit_bytes=44 << 20
        ),
        name="mixing",
    )(
        *(
            pltpu.with_memory_space_constraint(x, pltpu.HBM)
            for x in (
                features[0], key_proj[0], query_proj[0], log_decay[0], doc_start, loss_weight,
                target[0],
            )
        )
    )
    stored = pl.pallas_call(
        store_kernel,
        out_shape=tuple(jax.ShapeDtypeStruct(*shape) for shape in shapes),
        in_specs=(vmem,) * 5,
        out_specs=(pl.BlockSpec(memory_space=pl.ANY),) * 5,
        scratch_shapes=[pltpu.SemaphoreType.DMA((5,))],
        name="store",
    )(*(pltpu.with_memory_space_constraint(r, pltpu.VMEM) for r in results))
    return tuple(r[None] for r in stored)


def solution(mesh):
    placed = (
        P("dp", "seq", None),
        P("dp", "seq", None),
        P("dp", "seq", None),
        P("dp", None, "seq"),
        P("dp", "seq"),
        P("dp", "seq"),
        P("dp", "seq", None),
    )
    return jax.shard_map(
        body,
        mesh=mesh,
        in_specs=placed,
        out_specs=(
            P("dp", "seq", None),
            P("dp", "seq", None),
            P("dp", "seq", None),
            P("dp", "seq", None),
            P("dp", None, "seq"),
        ),
        check_vma=False,
    )
```

```python
import functools
import math

import jax
import jax.numpy as jnp
from jax import lax
from jax.experimental import pallas as pl
from jax.experimental.pallas import tpu as pltpu
from jax.sharding import PartitionSpec as P

F32 = jnp.float32
BF16 = jnp.bfloat16
MESH = pl.DeviceIdType.MESH
CHUNK = 128
EARLY = 3
SUM_AT = 4
BEHIND = 4
RAW_F = ((2, 4), (8, 11), (4, 10))
RAW_B = ((3, 13), (1, 7), (0, 3))
DETOUR_F = ((0, 15), (3, 15), (5, 16))
DETOUR_B = ((0, 0), (0, 0), (10, 12))
LAG_DF = (10, 8, 5, 7)
LAG_DB = (5, 2, 2, 9)
LEAD = (10, 14, 13, 16)
LAG_Y = (11, 12, 11, 4)
LAG_Z = (26, 27, 21, 9)
LAG_B = (31, 34, 34, 19)


def mm(a, b):
    return jnp.dot(a, b, preferred_element_type=F32)


def mm_nt(a, b):
    return lax.dot_general(a, b, (((1,), (1,)), ((), ())), preferred_element_type=F32)


def split(x):
    hi = x.astype(BF16)
    lo = (x - hi.astype(F32)).astype(BF16)
    return hi, lo


def kernel(
    n_seq, n_dp, heads,
    f_hbm, k_hbm, q_hbm, ld_hbm, ds_hbm, w_hbm, t_hbm,
    out_ref, gf_ref, gk_ref, gq_ref, gd_ref,
    xf_send, xf_recv, zf_send, zf_recv, rf_send, xb_send, xb_recv, zb_send, zb_recv, rb_send,
    before_s, adjoint_s, raw_recv, via_recv, g_send, g_recv, g_diag,
    rise_s, inv_s, y_s, dl_s, lift_s,
    dmix_s, dmixt_s, dq_s, dk_s, gk_s, rt_s, ex_s,
    wown, wdp, wrow, wside, wpair, wup, wdown, wlow, whigh, om_s,
    f_ref, k_ref, q_ref, ld_ref, ds_ref, w_ref, t_ref, in_sem,
    xfs, xfr, zfs, zfr, rfs, rfr, xbs, xbr, zbs, zbr, rbs, rbr, rws, rwr, vis, vir, vos, wds, wdr, ones, oner,
):
    length, width = f_ref.shape
    state = k_ref.shape[1]
    head_size = width // heads
    chunks = width // CHUNK
    per_chunk = CHUNK // head_size
    sigma = 1.0 / math.sqrt(state * length)

    me = lax.axis_index("seq")
    row = lax.axis_index("dp")
    pair = me // 2
    pairs = n_seq // 2
    is_odd = me % 2
    odd = is_odd == 1
    partner = me + 1 - 2 * is_odd

    fetches = [
        pltpu.make_async_copy(src, dst, in_sem.at[i])
        for i, (src, dst) in enumerate(
            [
                (ld_hbm, ld_ref), (ds_hbm, ds_ref), (w_hbm, w_ref), (k_hbm, k_ref),
                (q_hbm, q_ref), (f_hbm, f_ref), (t_hbm, t_ref),
            ]
        )
    ]
    for fetch in fetches:
        fetch.start()
    barrier = pltpu.get_barrier_semaphore()

    def greet(target):
        pl.semaphore_signal(barrier, inc=1, device_id=target, device_id_type=MESH)

    def greet_dp(d, _):
        greet({"dp": (row + d) % n_dp})
        return 0

    has_low = pair > 0
    has_high = pair < pairs - 1
    greet({"seq": partner})

    @pl.when(has_low)
    def _():
        greet({"seq": me - 2})

    @pl.when(has_high)
    def _():
        greet({"seq": me + 2})

    even = is_odd == 0
    diag = me - 1 + 2 * is_odd
    has_diag = (odd & has_high) | (even & has_low)

    @pl.when(has_diag)
    def _():
        greet({"seq": diag})

    lax.fori_loop(1, n_dp, greet_dp, 0)
    greeters = n_dp + sum(flag.astype(jnp.int32) for flag in (has_low, has_high, has_diag))

    for fetch in fetches[:5]:
        fetch.wait()
    wown[...] = jnp.broadcast_to(jnp.sum(w_ref[...], axis=1, keepdims=True), wown.shape)

    starts = ds_ref[...].astype(F32)
    table = jnp.concatenate(
        [
            ld_ref[...],
            jnp.broadcast_to(starts, (8, length)),
            jnp.broadcast_to(w_ref[...], (8, length)),
            jnp.zeros((128 - heads - 16, length), F32),
        ],
        axis=0,
    )
    rows_i = lax.broadcasted_iota(jnp.int32, (length, length), 0)
    cols_i = lax.broadcasted_iota(jnp.int32, (length, length), 1)
    lower = (rows_i >= cols_i).astype(F32).astype(BF16)
    upper = (rows_i <= cols_i).astype(F32).astype(BF16)
    eye = (rows_i == cols_i).astype(F32).astype(BF16)
    eye_n = eye[:state, :state]
    table_hi, table_lo = split(table)
    cumulative = mm_nt(lower, table_hi) + mm_nt(lower, table_lo)
    turned = mm_nt(eye, table_hi) + mm_nt(eye, table_lo)
    seg_col = cumulative[:, heads:heads + 1]
    seg_row = mm(jnp.broadcast_to(starts, (8, length)).astype(BF16), upper)[0:1]
    last_seg = jnp.sum(starts, axis=1, keepdims=True)
    tail_row = (seg_row == last_seg).astype(F32)
    tail_col = (seg_col == last_seg).astype(F32)
    open_row = (seg_row == 0.0).astype(F32)
    open_col = (seg_col == 0.0).astype(F32)
    whole_block = (last_seg == 0.0).astype(F32)
    run_hi, run_lo = split(cumulative)

    keys = k_ref[...]
    queries = q_ref[...]
    keys_t = (mm_nt(eye_n, keys) * tail_row).astype(BF16)
    queries_t = (mm_nt(eye_n, queries) * open_row).astype(BF16)
    keys_tail = (keys.astype(F32) * tail_col).astype(BF16)
    queries_open = (queries.astype(F32) * open_col).astype(BF16)

    head_i = lax.broadcasted_iota(jnp.int32, (128, CHUNK), 0)
    lane_h = lax.broadcasted_iota(jnp.int32, (128, CHUNK), 1) // head_size

    def spread(c):
        return (head_i == lane_h + c * per_chunk).astype(F32).astype(BF16)

    def lanes(c):
        return pl.ds(pl.multiple_of(c * CHUNK, CHUNK), CHUNK)

    part = state // 2
    mine = pl.ds(pl.multiple_of(is_odd * part, part), part)
    theirs = pl.ds(pl.multiple_of((1 - is_odd) * part, part), part)

    def remote(src, dst, ss, rs, c, target):
        return pltpu.make_async_remote_copy(
            src_ref=src, dst_ref=dst, send_sem=ss.at[c], recv_sem=rs.at[c],
            device_id={"seq": target}, device_id_type=MESH,
        )

    def xf(c):
        return remote(xf_send.at[c, theirs], xf_recv.at[c], xfs, xfr, c, partner)

    def xb(c):
        return remote(xb_send.at[c, theirs], xb_recv.at[c], xbs, xbr, c, partner)

    def zf(c):
        return remote(zf_send.at[c], zf_recv.at[c], zfs, zfr, c, me + 2)

    def zb(c):
        return remote(zb_send.at[c], zb_recv.at[c], zbs, zbr, c, me - 2)

    def rf(c):
        return remote(rf_send.at[c], before_s.at[c, mine], rfs, rfr, c, partner)

    def rb(c):
        return remote(rb_send.at[c], adjoint_s.at[c, mine], rbs, rbr, c, partner)

    def single(src, dst, i, target):
        return pltpu.make_async_remote_copy(
            src_ref=src, dst_ref=dst, send_sem=ones.at[i], recv_sem=oner.at[i],
            device_id={"seq": target}, device_id_type=MESH,
        )

    def look_up(table, at, size, generic):
        if len(table) != size:
            return jnp.int32(generic)
        found = jnp.int32(0)
        for i, n in enumerate(table):
            found = jnp.where(at == i, n * chunks // 16, found)
        return found

    def raw(src, c):
        return remote(src.at[c, theirs], raw_recv.at[c], rws, rwr, c, diag)

    def via(src, c):
        return remote(src.at[c], via_recv.at[c], vis, vir, c, partner)

    def on_f(c):
        return remote(via_recv.at[c], before_s.at[c, theirs], vos, rfr, c, me + 2)

    def on_b(c):
        return remote(via_recv.at[c], adjoint_s.at[c, theirs], vos, rbr, c, me - 2)

    def within(c, table, at):
        inside = c < 0
        if len(table) == pairs - 1:
            for i, (low, high) in enumerate(table):
                if low < high:
                    inside = inside | (
                        (at == i) & (c >= low * chunks // 16) & (c < high * chunks // 16)
                    )
        return inside

    def raw_f_out(c):
        return odd & within(c, RAW_F, pair)

    def raw_f_pass(c):
        return even & within(c, RAW_F, pair)

    def raw_f_in(c):
        return even & within(c, RAW_F, pair - 1)

    def raw_b_out(c):
        return even & within(c, RAW_B, pair - 1)

    def raw_b_pass(c):
        return odd & within(c, RAW_B, pair - 1)

    def raw_b_in(c):
        return odd & within(c, RAW_B, pair)

    def via_f_out(c):
        return odd & within(c, DETOUR_F, pair)

    def via_f_on(c):
        return even & within(c, DETOUR_F, pair)

    def via_f_skip(c):
        return odd & within(c, DETOUR_F, pair - 1)

    def via_b_out(c):
        return even & within(c, DETOUR_B, pair - 1)

    def via_b_on(c):
        return odd & within(c, DETOUR_B, pair - 1)

    def via_b_skip(c):
        return even & within(c, DETOUR_B, pair)

    to_next = even | has_high
    from_next = odd | has_high
    to_last = odd | has_low
    from_last = even | has_low

    def w_dp(d):
        return pltpu.make_async_remote_copy(
            src_ref=wrow, dst_ref=wdp.at[d - 1], send_sem=wds.at[d - 1], recv_sem=wdr.at[d - 1],
            device_id={"dp": (row + d) % n_dp}, device_id_type=MESH,
        )

    chunk_i = lax.broadcasted_iota(jnp.int32, (chunks, 128), 0)
    of_chunk = lax.broadcasted_iota(jnp.int32, (chunks, 128), 1) // per_chunk
    of_lane = (head_i % per_chunk == lane_h).astype(F32).astype(BF16)

    def pick(part):
        last = jnp.broadcast_to(part[length - 1:length].astype(F32), (chunks, 128))
        return mm(jnp.where(of_chunk == chunk_i, last, 0.0).astype(BF16), of_lane)

    g_send[...] = jnp.exp(pick(run_hi) + pick(run_lo)) * whole_block

    def fresh_step(c, _):
        e = spread(c)
        run_x = mm(run_hi, e) + mm(run_lo, e)
        rise = jnp.exp(run_x)
        inv = jnp.exp(-run_x)
        lifted = (f_ref[:, lanes(c)].astype(F32) * inv).astype(BF16)
        xf_send[c] = mm(keys_t, lifted) * (rise[length - 1:length] * sigma)
        rise_s[c] = rise
        inv_s[c] = inv
        lift_s[c] = lifted
        return 0

    def send_fresh(c, _):
        @pl.when(to_next & ~raw_f_out(c))
        def _():
            xf(c).start()

        @pl.when(raw_f_out(c))
        def _():
            raw(xf_send, c).start()

        return 0

    def fresh_and_send(c, _):
        fresh_step(c, 0)
        send_fresh(c, 0)
        return 0

    def start_w(d, _):
        w_dp(d).start()
        return 0

    linked = (rows_i >= cols_i) & (seg_col == seg_row)
    linked_t = (rows_i <= cols_i) & (seg_col == seg_row)
    fetches[5].wait()
    first = min(EARLY, chunks)
    lax.fori_loop(0, first, fresh_step, 0)
    mixing = jnp.where(linked, mm_nt(queries, keys) * sigma, 0.0).astype(BF16)
    mixing_t = jnp.where(linked_t, mm_nt(keys, queries) * sigma, 0.0).astype(BF16)
    dmix_s[...] = jnp.zeros_like(dmix_s)
    dmixt_s[...] = jnp.zeros_like(dmixt_s)
    dq_s[...] = jnp.zeros_like(dq_s)
    dk_s[...] = jnp.zeros_like(dk_s)
    rt_s[...] = jnp.zeros_like(rt_s)
    ex_s[...] = jnp.zeros_like(ex_s)

    @pl.when(pair == 0)
    def _():
        zf_recv[...] = jnp.zeros_like(zf_recv)
        wlow[...] = jnp.zeros_like(wlow)

        @pl.when(even)
        def _():
            before_s[...] = jnp.zeros_like(before_s)

    @pl.when(pair == pairs - 1)
    def _():
        zb_recv[...] = jnp.zeros_like(zb_recv)
        whigh[...] = jnp.zeros_like(whigh)

        @pl.when(odd)
        def _():
            adjoint_s[...] = jnp.zeros_like(adjoint_s)

    lead = jnp.maximum(first, look_up(LEAD, pair, pairs, chunks))
    lag_y = look_up(LAG_Y, pair, pairs, 0)
    sum_at = min(SUM_AT, chunks - 1)
    generic_lag = jnp.minimum(chunks, 3 + 5 * (pairs - 1 - pair))
    lag_z = jnp.maximum(look_up(LAG_Z, pair, pairs, generic_lag), jnp.maximum(lag_y, sum_at))
    lag_v = lag_z + look_up(LAG_DB, pair, pairs, 0)
    lag_u = look_up(LAG_DF, pair, pairs, 0)
    lag_b = jnp.maximum(look_up(LAG_B, pair, pairs, generic_lag), lag_v)

    pl.semaphore_wait(barrier, greeters)
    single(g_send, g_recv, 0, partner).start()
    single(wown, wside, 1, partner).start()

    @pl.when(has_diag)
    def _():
        single(g_send, g_diag, 4, diag).start()

    lax.fori_loop(0, first, send_fresh, 0)

    lax.fori_loop(first, lead, fresh_and_send, 0)
    single(wown, wside, 1, partner).wait_recv()
    wrow[...] = wown[...] + wside[...]
    lax.fori_loop(1, n_dp, start_w, 0)
    single(g_send, g_recv, 0, partner).wait_recv()

    @pl.when(has_diag)
    def _():
        single(g_send, g_diag, 4, diag).wait_recv()

    fetches[6].wait()
    weight = turned[:, heads + 8:heads + 9]

    def add_w(d, total):
        w_dp(d).wait_recv()
        return total + wdp[d - 1]

    def carry_forward(c):
        @pl.when(c == sum_at)
        def _():
            wpair[...] = lax.fori_loop(1, n_dp, add_w, wrow[...])

            @pl.when(has_low)
            def _():
                single(wup, wlow, 2, me).wait_recv()

            wup[...] = wlow[...] + wpair[...]

            @pl.when(has_high)
            def _():
                single(wup, wlow, 2, me + 2).start()

        @pl.when(has_low)
        def _():
            zf(c).wait_recv()

        @pl.when(from_next & ~raw_f_pass(c))
        def _():
            xf(c).wait_recv()

        @pl.when(raw_f_in(c))
        def _():
            raw(xf_send, c).wait_recv()

        own_keep = g_send[pl.ds(c, 1), :]
        other_keep = g_recv[pl.ds(c, 1), :]
        own = xf_send[c, mine]
        other = xf_recv[c]
        carried = zf_recv[c]
        diag_keep = g_diag[pl.ds(c, 1), :]
        entry = jnp.where(raw_f_in(c), raw_recv[c] + diag_keep * carried, carried)
        middle = jnp.where(odd, other, own) + jnp.where(odd, other_keep, own_keep) * entry
        onward = jnp.where(odd, own, other) + jnp.where(odd, own_keep, other_keep) * middle
        zf_send[c] = jnp.where(raw_f_pass(c), middle, onward)

        @pl.when(has_high)
        def _():
            zf(c).start()

        rf_send[c] = jnp.where(odd, entry, middle)

        @pl.when(from_last & ~via_f_skip(c))
        def _():
            rf(c).start()

        @pl.when(via_f_out(c))
        def _():
            via(zf_send, c).start()

        before_s[c, mine] = jnp.where(odd, middle, entry)

    def pass_forward(c):
        @pl.when(via_f_on(c))
        def _():
            via(zf_send, c).wait_recv()
            on_f(c).start()

    def pass_backward(c):
        @pl.when(via_b_on(c))
        def _():
            via(zb_send, c).wait_recv()
            on_b(c).start()

    def forward_step(c):
        @pl.when(to_last)
        def _():
            rf(c).wait_recv()

        before_h = before_s[c].astype(BF16)
        rise = rise_s[c]
        lifted = lift_s[c]
        y = rise * (mm(mixing, lifted) + mm(queries_open, before_h))
        grad = weight * (y - t_ref[:, lanes(c)].astype(F32))
        z = (grad * rise).astype(BF16)
        xb_send[c] = mm(queries_t, z)

        @pl.when(to_last & ~raw_b_out(c))
        def _():
            xb(c).start()

        @pl.when(raw_b_out(c))
        def _():
            raw(xb_send, c).start()

        out_ref[:, lanes(c)] = y.astype(BF16)
        y_s[c] = grad * y
        dq_s[...] += mm_nt(z, before_h)
        dmix_s[...] += mm_nt(z, lifted)
        dmixt_s[...] += mm_nt(lifted, z)
        dl_s[c] = mm(mixing_t, z)

    def sent_forward(c):
        @pl.when(to_next & ~raw_f_out(c))
        def _():
            xf(c).wait_send()

        @pl.when(raw_f_out(c))
        def _():
            raw(xf_send, c).wait_send()

        @pl.when(from_last & ~via_f_skip(c))
        def _():
            rf(c).wait_send()

        @pl.when(via_f_out(c))
        def _():
            via(zf_send, c).wait_send()

        @pl.when(via_f_on(c))
        def _():
            on_f(c).wait_send()

        @pl.when(has_high)
        def _():
            zf(c).wait_send()

    def sent_backward(c):
        @pl.when(to_last & ~raw_b_out(c))
        def _():
            xb(c).wait_send()

        @pl.when(raw_b_out(c))
        def _():
            raw(xb_send, c).wait_send()

        @pl.when(from_next & ~via_b_skip(c))
        def _():
            rb(c).wait_send()

        @pl.when(via_b_out(c))
        def _():
            via(zb_send, c).wait_send()

        @pl.when(via_b_on(c))
        def _():
            on_b(c).wait_send()

        @pl.when(has_low)
        def _():
            zb(c).wait_send()

    def carry_backward(c):
        @pl.when(has_high)
        def _():
            zb(c).wait_recv()

        @pl.when(from_last & ~raw_b_pass(c))
        def _():
            xb(c).wait_recv()

        @pl.when(raw_b_in(c))
        def _():
            raw(xb_send, c).wait_recv()

        own_keep = g_send[pl.ds(c, 1), :]
        other_keep = g_recv[pl.ds(c, 1), :]
        own = xb_send[c, mine]
        other = xb_recv[c]
        carried = zb_recv[c]
        diag_keep = g_diag[pl.ds(c, 1), :]
        entry = jnp.where(raw_b_in(c), raw_recv[c] + diag_keep * carried, carried)
        middle = jnp.where(odd, own, other) + jnp.where(odd, own_keep, other_keep) * entry
        onward = jnp.where(odd, other, own) + jnp.where(odd, other_keep, own_keep) * middle
        zb_send[c] = jnp.where(raw_b_pass(c), middle, onward)

        @pl.when(has_low)
        def _():
            zb(c).start()

        rb_send[c] = jnp.where(odd, middle, entry)

        @pl.when(from_next & ~via_b_skip(c))
        def _():
            rb(c).start()

        @pl.when(via_b_out(c))
        def _():
            via(zb_send, c).start()

        adjoint_s[c, mine] = jnp.where(odd, entry, middle)

        @pl.when(c == 0)
        def _():
            @pl.when(has_high)
            def _():
                single(wdown, whigh, 3, me).wait_recv()

            wdown[...] = whigh[...] + wpair[...]

            @pl.when(has_low)
            def _():
                single(wdown, whigh, 3, me - 2).start()

            om_s[...] = (length * n_seq * n_dp) / (wlow[...] + wpair[...] + whigh[...])

    def backward_step(c):
        @pl.when(to_next)
        def _():
            rb(c).wait_recv()

        over_mean = om_s[0:1, 0:1]
        e = spread(c)
        gain = rise_s[c, length - 1:length, :]
        adjoint = adjoint_s[c] * over_mean
        scaled = (adjoint * (gain * sigma)).astype(BF16)
        d_feature = inv_s[c] * (dl_s[c] * over_mean + mm(keys_tail, scaled))
        gf_ref[:, lanes(c)] = d_feature.astype(BF16)
        change = y_s[c] * over_mean - f_ref[:, lanes(c)].astype(F32) * d_feature
        change_hi, change_lo = split(change)
        rt_s[...] += mm_nt(e, change_hi) + mm_nt(e, change_lo)
        dk_s[...] += mm_nt(lift_s[c], scaled)
        after = xf_send[c] + g_send[pl.ds(c, 1), :] * before_s[c]
        end_hi, end_lo = split(adjoint * after)
        ex_s[...] += mm_nt(e, end_hi) + mm_nt(e, end_lo)
        sent_forward(c)

        @pl.when(c >= BEHIND)
        def _():
            sent_backward(c - BEHIND)

    def finish_scores():
        over_mean = om_s[0:1, 0:1]
        d_scores = (jnp.where(linked, dmix_s[...], 0.0) * (over_mean * sigma)).astype(BF16)
        d_scores_t = (jnp.where(linked_t, dmixt_s[...], 0.0) * (over_mean * sigma)).astype(BF16)
        gq_ref[...] = (mm(d_scores, keys) + (open_col * over_mean) * dq_s[...]).astype(BF16)
        gk_s[...] = mm(d_scores_t, queries)

    def step(i, _):
        @pl.when(i + lead < chunks)
        def _():
            fresh_and_send(i + lead, 0)

        @pl.when(i < chunks)
        def _():
            carry_forward(i)

        @pl.when((i >= lag_u) & (i < lag_u + chunks))
        def _():
            pass_forward(i - lag_u)

        @pl.when((i >= lag_y) & (i < lag_y + chunks))
        def _():
            forward_step(i - lag_y)

        @pl.when((i >= lag_z) & (i < lag_z + chunks))
        def _():
            carry_backward(i - lag_z)

        @pl.when((i >= lag_v) & (i < lag_v + chunks))
        def _():
            pass_backward(i - lag_v)

        @pl.when(i == jnp.maximum(chunks + lag_y, lag_z + 1))
        def _():
            finish_scores()

        @pl.when((i >= lag_b) & (i < lag_b + chunks))
        def _():
            backward_step(i - lag_b)

        return 0

    end = jnp.maximum(chunks + jnp.maximum(lag_b, jnp.maximum(lag_y + 1, lag_u)), lag_z + 2)
    lax.fori_loop(0, end, step, 0)

    gk_ref[...] = (gk_s[...] + tail_col * dk_s[...]).astype(BF16)
    rt_hi, rt_lo = split(rt_s[...])
    decay = mm(rt_hi, lower) + mm(rt_lo, lower) + jnp.sum(ex_s[...], axis=1, keepdims=True)
    gd_ref[...] = decay[:heads]

    def finish_step(c, _):
        sent_backward(c)
        return 0

    lax.fori_loop(max(chunks - BEHIND, 0), chunks, finish_step, 0)

    def finish_w(d, _):
        w_dp(d).wait_send()
        return 0

    lax.fori_loop(1, n_dp, finish_w, 0)
    single(g_send, g_recv, 0, partner).wait_send()

    @pl.when(has_diag)
    def _():
        single(g_send, g_diag, 4, diag).wait_send()
    single(wown, wside, 1, partner).wait_send()

    @pl.when(has_high)
    def _():
        single(wup, wlow, 2, me + 2).wait_send()

    @pl.when(has_low)
    def _():
        single(wdown, whigh, 3, me - 2).wait_send()


def store_kernel(*refs):
    count = len(refs) // 2
    sem = refs[-1]
    copies = [
        pltpu.make_async_copy(refs[i], refs[count + i], sem.at[i]) for i in range(count)
    ]
    for copy in copies:
        copy.start()
    for copy in copies:
        copy.wait()


def body(features, key_proj, query_proj, log_decay, doc_start, loss_weight, target):
    n_seq, n_dp = lax.axis_size("seq"), lax.axis_size("dp")
    length, width = features.shape[1:]
    state = key_proj.shape[2]
    heads = log_decay.shape[1]
    chunks = width // CHUNK
    vmem = pl.BlockSpec(memory_space=pltpu.VMEM)
    big = (chunks, length, CHUNK)
    small = (chunks, state, CHUNK)
    half = (chunks, state // 2, CHUNK)
    scratch = [
        pltpu.VMEM(small, F32), pltpu.VMEM(half, F32), pltpu.VMEM(half, F32),
        pltpu.VMEM(half, F32), pltpu.VMEM(half, F32),
        pltpu.VMEM(small, F32), pltpu.VMEM(half, F32), pltpu.VMEM(half, F32),
        pltpu.VMEM(half, F32), pltpu.VMEM(half, F32),
        pltpu.VMEM(small, F32), pltpu.VMEM(small, F32),
        pltpu.VMEM(half, F32), pltpu.VMEM(half, F32), pltpu.VMEM((chunks, CHUNK), F32),
        pltpu.VMEM((chunks, CHUNK), F32), pltpu.VMEM((chunks, CHUNK), F32),
        pltpu.VMEM(big, F32), pltpu.VMEM(big, F32), pltpu.VMEM(big, F32), pltpu.VMEM(big, F32),
        pltpu.VMEM(big, BF16),
        pltpu.VMEM((length, length), F32), pltpu.VMEM((length, length), F32),
        pltpu.VMEM((length, state), F32), pltpu.VMEM((length, state), F32),
        pltpu.VMEM((length, state), F32), pltpu.VMEM((128, length), F32), pltpu.VMEM((128, state), F32),
        pltpu.VMEM((8, 128), F32), pltpu.VMEM((n_dp - 1, 8, 128), F32),
    ]
    scratch += [pltpu.VMEM((8, 128), F32)] * 8
    scratch += [
        pltpu.VMEM((length, width), BF16), pltpu.VMEM((length, state), BF16),
        pltpu.VMEM((length, state), BF16), pltpu.VMEM((heads, length), F32),
        pltpu.VMEM((1, length), jnp.int32), pltpu.VMEM((1, length), F32),
        pltpu.VMEM((length, width), BF16), pltpu.SemaphoreType.DMA((7,)),
    ]
    scratch += [pltpu.SemaphoreType.DMA((chunks,))] * 17
    scratch += [pltpu.SemaphoreType.DMA((n_dp - 1,))] * 2
    scratch += [pltpu.SemaphoreType.DMA((5,))] * 2
    shapes = (
        ((length, width), BF16),
        ((length, width), BF16),
        ((length, state), BF16),
        ((length, state), BF16),
        ((heads, length), F32),
    )
    results = pl.pallas_call(
        functools.partial(kernel, n_seq, n_dp, heads),
        out_shape=tuple(pltpu.VMEM(*shape) for shape in shapes),
        in_specs=[pl.BlockSpec(memory_space=pltpu.HBM)] * 7,
        out_specs=(vmem,) * 5,
        scratch_shapes=scratch,
        compiler_params=pltpu.CompilerParams(
            collective_id=0, has_side_effects=True, vmem_limit_bytes=44 << 20
        ),
        name="mixing",
    )(
        *(
            pltpu.with_memory_space_constraint(x, pltpu.HBM)
            for x in (
                features[0], key_proj[0], query_proj[0], log_decay[0], doc_start, loss_weight,
                target[0],
            )
        )
    )
    stored = pl.pallas_call(
        store_kernel,
        out_shape=tuple(jax.ShapeDtypeStruct(*shape) for shape in shapes),
        in_specs=(vmem,) * 5,
        out_specs=(pl.BlockSpec(memory_space=pl.ANY),) * 5,
        scratch_shapes=[pltpu.SemaphoreType.DMA((5,))],
        name="store",
    )(*(pltpu.with_memory_space_constraint(r, pltpu.VMEM) for r in results))
    return tuple(r[None] for r in stored)


def solution(mesh):
    placed = (
        P("dp", "seq", None),
        P("dp", "seq", None),
        P("dp", "seq", None),
        P("dp", None, "seq"),
        P("dp", "seq"),
        P("dp", "seq"),
        P("dp", "seq", None),
    )
    return jax.shard_map(
        body,
        mesh=mesh,
        in_specs=placed,
        out_specs=(
            P("dp", "seq", None),
            P("dp", "seq", None),
            P("dp", "seq", None),
            P("dp", "seq", None),
            P("dp", None, "seq"),
        ),
        check_vma=False,
    )
```

```python
import functools
import math

import jax
import jax.numpy as jnp
from jax import lax
from jax.experimental import pallas as pl
from jax.experimental.pallas import tpu as pltpu
from jax.sharding import PartitionSpec as P

F32 = jnp.float32
BF16 = jnp.bfloat16
MESH = pl.DeviceIdType.MESH
CHUNK = 128
EARLY = 3
SUM_AT = 4
BEHIND = 4
RAW_F = ((9, 10), (9, 13), (1, 13))
RAW_B = ((0, 9), (2, 10), (0, 5))
DETOUR_F = ((7, 16), (5, 16), (6, 16))
DETOUR_B = ((0, 0), (0, 0), (0, 0))
LAG_DF = (7, 9, 4, 1)
LAG_DB = (2, 7, 2, 4)
LEAD = (11, 12, 14, 16)
LAG_Y = (15, 14, 10, 5)
LAG_Z = (28, 25, 20, 12)
LAG_B = (33, 34, 33, 20)


def mm(a, b):
    return jnp.dot(a, b, preferred_element_type=F32)


def mm_nt(a, b):
    return lax.dot_general(a, b, (((1,), (1,)), ((), ())), preferred_element_type=F32)


def split(x):
    hi = x.astype(BF16)
    lo = (x - hi.astype(F32)).astype(BF16)
    return hi, lo


def kernel(
    n_seq, n_dp, heads,
    f_hbm, k_hbm, q_hbm, ld_hbm, ds_hbm, w_hbm, t_hbm,
    out_ref, gf_ref, gk_ref, gq_ref, gd_ref,
    xf_send, xf_recv, zf_send, zf_recv, rf_send, xb_send, xb_recv, zb_send, zb_recv, rb_send,
    before_s, adjoint_s, raw_recv, via_recv, g_send, g_recv, g_diag,
    rise_s, inv_s, y_s, dl_s, lift_s,
    dmix_s, dmixt_s, dq_s, dk_s, gk_s, rt_s, ex_s,
    wown, wdp, wrow, wside, wpair, wup, wdown, wlow, whigh, om_s,
    f_ref, k_ref, q_ref, ld_ref, ds_ref, w_ref, t_ref, in_sem,
    xfs, xfr, zfs, zfr, rfs, rfr, xbs, xbr, zbs, zbr, rbs, rbr, rws, rwr, vis, vir, vos, wds, wdr, ones, oner,
):
    length, width = f_ref.shape
    state = k_ref.shape[1]
    head_size = width // heads
    chunks = width // CHUNK
    per_chunk = CHUNK // head_size
    sigma = 1.0 / math.sqrt(state * length)

    me = lax.axis_index("seq")
    row = lax.axis_index("dp")
    pair = me // 2
    pairs = n_seq // 2
    is_odd = me % 2
    odd = is_odd == 1
    partner = me + 1 - 2 * is_odd

    fetches = [
        pltpu.make_async_copy(src, dst, in_sem.at[i])
        for i, (src, dst) in enumerate(
            [
                (ld_hbm, ld_ref), (ds_hbm, ds_ref), (w_hbm, w_ref), (k_hbm, k_ref),
                (q_hbm, q_ref), (f_hbm, f_ref), (t_hbm, t_ref),
            ]
        )
    ]
    for fetch in fetches:
        fetch.start()
    barrier = pltpu.get_barrier_semaphore()

    def greet(target):
        pl.semaphore_signal(barrier, inc=1, device_id=target, device_id_type=MESH)

    def greet_dp(d, _):
        greet({"dp": (row + d) % n_dp})
        return 0

    has_low = pair > 0
    has_high = pair < pairs - 1
    greet({"seq": partner})

    @pl.when(has_low)
    def _():
        greet({"seq": me - 2})

    @pl.when(has_high)
    def _():
        greet({"seq": me + 2})

    even = is_odd == 0
    diag = me - 1 + 2 * is_odd
    has_diag = (odd & has_high) | (even & has_low)

    @pl.when(has_diag)
    def _():
        greet({"seq": diag})

    lax.fori_loop(1, n_dp, greet_dp, 0)
    greeters = n_dp + sum(flag.astype(jnp.int32) for flag in (has_low, has_high, has_diag))

    for fetch in fetches[:5]:
        fetch.wait()
    wown[...] = jnp.broadcast_to(jnp.sum(w_ref[...], axis=1, keepdims=True), wown.shape)

    starts = ds_ref[...].astype(F32)
    table = jnp.concatenate(
        [
            ld_ref[...],
            jnp.broadcast_to(starts, (8, length)),
            jnp.broadcast_to(w_ref[...], (8, length)),
            jnp.zeros((128 - heads - 16, length), F32),
        ],
        axis=0,
    )
    rows_i = lax.broadcasted_iota(jnp.int32, (length, length), 0)
    cols_i = lax.broadcasted_iota(jnp.int32, (length, length), 1)
    lower = (rows_i >= cols_i).astype(F32).astype(BF16)
    upper = (rows_i <= cols_i).astype(F32).astype(BF16)
    eye = (rows_i == cols_i).astype(F32).astype(BF16)
    eye_n = eye[:state, :state]
    table_hi, table_lo = split(table)
    cumulative = mm_nt(lower, table_hi) + mm_nt(lower, table_lo)
    turned = mm_nt(eye, table_hi) + mm_nt(eye, table_lo)
    seg_col = cumulative[:, heads:heads + 1]
    seg_row = mm(jnp.broadcast_to(starts, (8, length)).astype(BF16), upper)[0:1]
    last_seg = jnp.sum(starts, axis=1, keepdims=True)
    tail_row = (seg_row == last_seg).astype(F32)
    tail_col = (seg_col == last_seg).astype(F32)
    open_row = (seg_row == 0.0).astype(F32)
    open_col = (seg_col == 0.0).astype(F32)
    whole_block = (last_seg == 0.0).astype(F32)
    run_hi, run_lo = split(cumulative)

    keys = k_ref[...]
    queries = q_ref[...]
    keys_t = (mm_nt(eye_n, keys) * tail_row).astype(BF16)
    queries_t = (mm_nt(eye_n, queries) * open_row).astype(BF16)
    keys_tail = (keys.astype(F32) * tail_col).astype(BF16)
    queries_open = (queries.astype(F32) * open_col).astype(BF16)

    head_i = lax.broadcasted_iota(jnp.int32, (128, CHUNK), 0)
    lane_h = lax.broadcasted_iota(jnp.int32, (128, CHUNK), 1) // head_size

    def spread(c):
        return (head_i == lane_h + c * per_chunk).astype(F32).astype(BF16)

    def lanes(c):
        return pl.ds(pl.multiple_of(c * CHUNK, CHUNK), CHUNK)

    part = state // 2
    mine = pl.ds(pl.multiple_of(is_odd * part, part), part)
    theirs = pl.ds(pl.multiple_of((1 - is_odd) * part, part), part)

    def remote(src, dst, ss, rs, c, target):
        return pltpu.make_async_remote_copy(
            src_ref=src, dst_ref=dst, send_sem=ss.at[c], recv_sem=rs.at[c],
            device_id={"seq": target}, device_id_type=MESH,
        )

    def xf(c):
        return remote(xf_send.at[c, theirs], xf_recv.at[c], xfs, xfr, c, partner)

    def xb(c):
        return remote(xb_send.at[c, theirs], xb_recv.at[c], xbs, xbr, c, partner)

    def zf(c):
        return remote(zf_send.at[c], zf_recv.at[c], zfs, zfr, c, me + 2)

    def zb(c):
        return remote(zb_send.at[c], zb_recv.at[c], zbs, zbr, c, me - 2)

    def rf(c):
        return remote(rf_send.at[c], before_s.at[c, mine], rfs, rfr, c, partner)

    def rb(c):
        return remote(rb_send.at[c], adjoint_s.at[c, mine], rbs, rbr, c, partner)

    def single(src, dst, i, target):
        return pltpu.make_async_remote_copy(
            src_ref=src, dst_ref=dst, send_sem=ones.at[i], recv_sem=oner.at[i],
            device_id={"seq": target}, device_id_type=MESH,
        )

    def look_up(table, at, size, generic):
        if len(table) != size:
            return jnp.int32(generic)
        found = jnp.int32(0)
        for i, n in enumerate(table):
            found = jnp.where(at == i, n * chunks // 16, found)
        return found

    def raw(src, c):
        return remote(src.at[c, theirs], raw_recv.at[c], rws, rwr, c, diag)

    def via(src, c):
        return remote(src.at[c], via_recv.at[c], vis, vir, c, partner)

    def on_f(c):
        return remote(via_recv.at[c], before_s.at[c, theirs], vos, rfr, c, me + 2)

    def on_b(c):
        return remote(via_recv.at[c], adjoint_s.at[c, theirs], vos, rbr, c, me - 2)

    def within(c, table, at):
        inside = c < 0
        if len(table) == pairs - 1:
            for i, (low, high) in enumerate(table):
                if low < high:
                    inside = inside | (
                        (at == i) & (c >= low * chunks // 16) & (c < high * chunks // 16)
                    )
        return inside

    def raw_f_out(c):
        return odd & within(c, RAW_F, pair)

    def raw_f_pass(c):
        return even & within(c, RAW_F, pair)

    def raw_f_in(c):
        return even & within(c, RAW_F, pair - 1)

    def raw_b_out(c):
        return even & within(c, RAW_B, pair - 1)

    def raw_b_pass(c):
        return odd & within(c, RAW_B, pair - 1)

    def raw_b_in(c):
        return odd & within(c, RAW_B, pair)

    def via_f_out(c):
        return odd & within(c, DETOUR_F, pair)

    def via_f_on(c):
        return even & within(c, DETOUR_F, pair)

    def via_f_skip(c):
        return odd & within(c, DETOUR_F, pair - 1)

    def via_b_out(c):
        return even & within(c, DETOUR_B, pair - 1)

    def via_b_on(c):
        return odd & within(c, DETOUR_B, pair - 1)

    def via_b_skip(c):
        return even & within(c, DETOUR_B, pair)

    to_next = even | has_high
    from_next = odd | has_high
    to_last = odd | has_low
    from_last = even | has_low

    def w_dp(d):
        return pltpu.make_async_remote_copy(
            src_ref=wrow, dst_ref=wdp.at[d - 1], send_sem=wds.at[d - 1], recv_sem=wdr.at[d - 1],
            device_id={"dp": (row + d) % n_dp}, device_id_type=MESH,
        )

    chunk_i = lax.broadcasted_iota(jnp.int32, (chunks, 128), 0)
    of_chunk = lax.broadcasted_iota(jnp.int32, (chunks, 128), 1) // per_chunk
    of_lane = (head_i % per_chunk == lane_h).astype(F32).astype(BF16)

    def pick(part):
        last = jnp.broadcast_to(part[length - 1:length].astype(F32), (chunks, 128))
        return mm(jnp.where(of_chunk == chunk_i, last, 0.0).astype(BF16), of_lane)

    g_send[...] = jnp.exp(pick(run_hi) + pick(run_lo)) * whole_block

    def fresh_step(c, _):
        e = spread(c)
        run_x = mm(run_hi, e) + mm(run_lo, e)
        rise = jnp.exp(run_x)
        inv = jnp.exp(-run_x)
        lifted = (f_ref[:, lanes(c)].astype(F32) * inv).astype(BF16)
        xf_send[c] = mm(keys_t, lifted) * (rise[length - 1:length] * sigma)
        rise_s[c] = rise
        inv_s[c] = inv
        lift_s[c] = lifted
        return 0

    def send_fresh(c, _):
        @pl.when(to_next & ~raw_f_out(c))
        def _():
            xf(c).start()

        @pl.when(raw_f_out(c))
        def _():
            raw(xf_send, c).start()

        return 0

    def fresh_and_send(c, _):
        fresh_step(c, 0)
        send_fresh(c, 0)
        return 0

    def start_w(d, _):
        w_dp(d).start()
        return 0

    linked = (rows_i >= cols_i) & (seg_col == seg_row)
    linked_t = (rows_i <= cols_i) & (seg_col == seg_row)
    fetches[5].wait()
    first = min(EARLY, chunks)
    lax.fori_loop(0, first, fresh_step, 0)
    mixing = jnp.where(linked, mm_nt(queries, keys) * sigma, 0.0).astype(BF16)
    mixing_t = jnp.where(linked_t, mm_nt(keys, queries) * sigma, 0.0).astype(BF16)
    dmix_s[...] = jnp.zeros_like(dmix_s)
    dmixt_s[...] = jnp.zeros_like(dmixt_s)
    dq_s[...] = jnp.zeros_like(dq_s)
    dk_s[...] = jnp.zeros_like(dk_s)
    rt_s[...] = jnp.zeros_like(rt_s)
    ex_s[...] = jnp.zeros_like(ex_s)

    @pl.when(pair == 0)
    def _():
        zf_recv[...] = jnp.zeros_like(zf_recv)
        wlow[...] = jnp.zeros_like(wlow)

        @pl.when(even)
        def _():
            before_s[...] = jnp.zeros_like(before_s)

    @pl.when(pair == pairs - 1)
    def _():
        zb_recv[...] = jnp.zeros_like(zb_recv)
        whigh[...] = jnp.zeros_like(whigh)

        @pl.when(odd)
        def _():
            adjoint_s[...] = jnp.zeros_like(adjoint_s)

    lead = jnp.maximum(first, look_up(LEAD, pair, pairs, chunks))
    lag_y = look_up(LAG_Y, pair, pairs, 0)
    sum_at = min(SUM_AT, chunks - 1)
    generic_lag = jnp.minimum(chunks, 3 + 5 * (pairs - 1 - pair))
    lag_z = jnp.maximum(look_up(LAG_Z, pair, pairs, generic_lag), jnp.maximum(lag_y, sum_at))
    lag_v = lag_z + look_up(LAG_DB, pair, pairs, 0)
    lag_u = look_up(LAG_DF, pair, pairs, 0)
    lag_b = jnp.maximum(look_up(LAG_B, pair, pairs, generic_lag), lag_v)

    pl.semaphore_wait(barrier, greeters)
    single(g_send, g_recv, 0, partner).start()
    single(wown, wside, 1, partner).start()

    @pl.when(has_diag)
    def _():
        single(g_send, g_diag, 4, diag).start()

    lax.fori_loop(0, first, send_fresh, 0)

    lax.fori_loop(first, lead, fresh_and_send, 0)
    single(wown, wside, 1, partner).wait_recv()
    wrow[...] = wown[...] + wside[...]
    lax.fori_loop(1, n_dp, start_w, 0)
    single(g_send, g_recv, 0, partner).wait_recv()

    @pl.when(has_diag)
    def _():
        single(g_send, g_diag, 4, diag).wait_recv()

    fetches[6].wait()
    weight = turned[:, heads + 8:heads + 9]

    def add_w(d, total):
        w_dp(d).wait_recv()
        return total + wdp[d - 1]

    def carry_forward(c):
        @pl.when(c == sum_at)
        def _():
            wpair[...] = lax.fori_loop(1, n_dp, add_w, wrow[...])

            @pl.when(has_low)
            def _():
                single(wup, wlow, 2, me).wait_recv()

            wup[...] = wlow[...] + wpair[...]

            @pl.when(has_high)
            def _():
                single(wup, wlow, 2, me + 2).start()

        @pl.when(has_low)
        def _():
            zf(c).wait_recv()

        @pl.when(from_next & ~raw_f_pass(c))
        def _():
            xf(c).wait_recv()

        @pl.when(raw_f_in(c))
        def _():
            raw(xf_send, c).wait_recv()

        own_keep = g_send[pl.ds(c, 1), :]
        other_keep = g_recv[pl.ds(c, 1), :]
        own = xf_send[c, mine]
        other = xf_recv[c]
        carried = zf_recv[c]
        diag_keep = g_diag[pl.ds(c, 1), :]
        entry = jnp.where(raw_f_in(c), raw_recv[c] + diag_keep * carried, carried)
        middle = jnp.where(odd, other, own) + jnp.where(odd, other_keep, own_keep) * entry
        onward = jnp.where(odd, own, other) + jnp.where(odd, own_keep, other_keep) * middle
        zf_send[c] = jnp.where(raw_f_pass(c), middle, onward)

        @pl.when(has_high)
        def _():
            zf(c).start()

        rf_send[c] = jnp.where(odd, entry, middle)

        @pl.when(from_last & ~via_f_skip(c))
        def _():
            rf(c).start()

        @pl.when(via_f_out(c))
        def _():
            via(zf_send, c).start()

        before_s[c, mine] = jnp.where(odd, middle, entry)

    def pass_forward(c):
        @pl.when(via_f_on(c))
        def _():
            via(zf_send, c).wait_recv()
            on_f(c).start()

    def pass_backward(c):
        @pl.when(via_b_on(c))
        def _():
            via(zb_send, c).wait_recv()
            on_b(c).start()

    def forward_step(c):
        @pl.when(to_last)
        def _():
            rf(c).wait_recv()

        before_h = before_s[c].astype(BF16)
        rise = rise_s[c]
        lifted = lift_s[c]
        y = rise * (mm(mixing, lifted) + mm(queries_open, before_h))
        grad = weight * (y - t_ref[:, lanes(c)].astype(F32))
        z = (grad * rise).astype(BF16)
        xb_send[c] = mm(queries_t, z)

        @pl.when(to_last & ~raw_b_out(c))
        def _():
            xb(c).start()

        @pl.when(raw_b_out(c))
        def _():
            raw(xb_send, c).start()

        out_ref[:, lanes(c)] = y.astype(BF16)
        y_s[c] = grad * y
        dq_s[...] += mm_nt(z, before_h)
        dmix_s[...] += mm_nt(z, lifted)
        dmixt_s[...] += mm_nt(lifted, z)
        dl_s[c] = mm(mixing_t, z)

    def sent_forward(c):
        @pl.when(to_next & ~raw_f_out(c))
        def _():
            xf(c).wait_send()

        @pl.when(raw_f_out(c))
        def _():
            raw(xf_send, c).wait_send()

        @pl.when(from_last & ~via_f_skip(c))
        def _():
            rf(c).wait_send()

        @pl.when(via_f_out(c))
        def _():
            via(zf_send, c).wait_send()

        @pl.when(via_f_on(c))
        def _():
            on_f(c).wait_send()

        @pl.when(has_high)
        def _():
            zf(c).wait_send()

    def sent_backward(c):
        @pl.when(to_last & ~raw_b_out(c))
        def _():
            xb(c).wait_send()

        @pl.when(raw_b_out(c))
        def _():
            raw(xb_send, c).wait_send()

        @pl.when(from_next & ~via_b_skip(c))
        def _():
            rb(c).wait_send()

        @pl.when(via_b_out(c))
        def _():
            via(zb_send, c).wait_send()

        @pl.when(via_b_on(c))
        def _():
            on_b(c).wait_send()

        @pl.when(has_low)
        def _():
            zb(c).wait_send()

    def carry_backward(c):
        @pl.when(has_high)
        def _():
            zb(c).wait_recv()

        @pl.when(from_last & ~raw_b_pass(c))
        def _():
            xb(c).wait_recv()

        @pl.when(raw_b_in(c))
        def _():
            raw(xb_send, c).wait_recv()

        own_keep = g_send[pl.ds(c, 1), :]
        other_keep = g_recv[pl.ds(c, 1), :]
        own = xb_send[c, mine]
        other = xb_recv[c]
        carried = zb_recv[c]
        diag_keep = g_diag[pl.ds(c, 1), :]
        entry = jnp.where(raw_b_in(c), raw_recv[c] + diag_keep * carried, carried)
        middle = jnp.where(odd, own, other) + jnp.where(odd, own_keep, other_keep) * entry
        onward = jnp.where(odd, other, own) + jnp.where(odd, other_keep, own_keep) * middle
        zb_send[c] = jnp.where(raw_b_pass(c), middle, onward)

        @pl.when(has_low)
        def _():
            zb(c).start()

        rb_send[c] = jnp.where(odd, middle, entry)

        @pl.when(from_next & ~via_b_skip(c))
        def _():
            rb(c).start()

        @pl.when(via_b_out(c))
        def _():
            via(zb_send, c).start()

        adjoint_s[c, mine] = jnp.where(odd, entry, middle)

        @pl.when(c == 0)
        def _():
            @pl.when(has_high)
            def _():
                single(wdown, whigh, 3, me).wait_recv()

            wdown[...] = whigh[...] + wpair[...]

            @pl.when(has_low)
            def _():
                single(wdown, whigh, 3, me - 2).start()

            om_s[...] = (length * n_seq * n_dp) / (wlow[...] + wpair[...] + whigh[...])

    def backward_step(c):
        @pl.when(to_next)
        def _():
            rb(c).wait_recv()

        over_mean = om_s[0:1, 0:1]
        e = spread(c)
        gain = rise_s[c, length - 1:length, :]
        adjoint = adjoint_s[c] * over_mean
        scaled = (adjoint * (gain * sigma)).astype(BF16)
        d_feature = inv_s[c] * (dl_s[c] * over_mean + mm(keys_tail, scaled))
        gf_ref[:, lanes(c)] = d_feature.astype(BF16)
        change = y_s[c] * over_mean - f_ref[:, lanes(c)].astype(F32) * d_feature
        change_hi, change_lo = split(change)
        rt_s[...] += mm_nt(e, change_hi) + mm_nt(e, change_lo)
        dk_s[...] += mm_nt(lift_s[c], scaled)
        after = xf_send[c] + g_send[pl.ds(c, 1), :] * before_s[c]
        end_hi, end_lo = split(adjoint * after)
        ex_s[...] += mm_nt(e, end_hi) + mm_nt(e, end_lo)
        sent_forward(c)

        @pl.when(c >= BEHIND)
        def _():
            sent_backward(c - BEHIND)

    def finish_scores():
        over_mean = om_s[0:1, 0:1]
        d_scores = (jnp.where(linked, dmix_s[...], 0.0) * (over_mean * sigma)).astype(BF16)
        d_scores_t = (jnp.where(linked_t, dmixt_s[...], 0.0) * (over_mean * sigma)).astype(BF16)
        gq_ref[...] = (mm(d_scores, keys) + (open_col * over_mean) * dq_s[...]).astype(BF16)
        gk_s[...] = mm(d_scores_t, queries)

    def step(i, _):
        @pl.when(i + lead < chunks)
        def _():
            fresh_and_send(i + lead, 0)

        @pl.when(i < chunks)
        def _():
            carry_forward(i)

        @pl.when((i >= lag_u) & (i < lag_u + chunks))
        def _():
            pass_forward(i - lag_u)

        @pl.when((i >= lag_y) & (i < lag_y + chunks))
        def _():
            forward_step(i - lag_y)

        @pl.when((i >= lag_z) & (i < lag_z + chunks))
        def _():
            carry_backward(i - lag_z)

        @pl.when((i >= lag_v) & (i < lag_v + chunks))
        def _():
            pass_backward(i - lag_v)

        @pl.when(i == jnp.maximum(chunks + lag_y, lag_z + 1))
        def _():
            finish_scores()

        @pl.when((i >= lag_b) & (i < lag_b + chunks))
        def _():
            backward_step(i - lag_b)

        return 0

    end = jnp.maximum(chunks + jnp.maximum(lag_b, jnp.maximum(lag_y + 1, lag_u)), lag_z + 2)
    lax.fori_loop(0, end, step, 0)

    gk_ref[...] = (gk_s[...] + tail_col * dk_s[...]).astype(BF16)
    rt_hi, rt_lo = split(rt_s[...])
    decay = mm(rt_hi, lower) + mm(rt_lo, lower) + jnp.sum(ex_s[...], axis=1, keepdims=True)
    gd_ref[...] = decay[:heads]

    def finish_step(c, _):
        sent_backward(c)
        return 0

    lax.fori_loop(max(chunks - BEHIND, 0), chunks, finish_step, 0)

    def finish_w(d, _):
        w_dp(d).wait_send()
        return 0

    lax.fori_loop(1, n_dp, finish_w, 0)
    single(g_send, g_recv, 0, partner).wait_send()

    @pl.when(has_diag)
    def _():
        single(g_send, g_diag, 4, diag).wait_send()
    single(wown, wside, 1, partner).wait_send()

    @pl.when(has_high)
    def _():
        single(wup, wlow, 2, me + 2).wait_send()

    @pl.when(has_low)
    def _():
        single(wdown, whigh, 3, me - 2).wait_send()


def store_kernel(*refs):
    count = len(refs) // 2
    sem = refs[-1]
    copies = [
        pltpu.make_async_copy(refs[i], refs[count + i], sem.at[i]) for i in range(count)
    ]
    for copy in copies:
        copy.start()
    for copy in copies:
        copy.wait()


def body(features, key_proj, query_proj, log_decay, doc_start, loss_weight, target):
    n_seq, n_dp = lax.axis_size("seq"), lax.axis_size("dp")
    length, width = features.shape[1:]
    state = key_proj.shape[2]
    heads = log_decay.shape[1]
    chunks = width // CHUNK
    vmem = pl.BlockSpec(memory_space=pltpu.VMEM)
    big = (chunks, length, CHUNK)
    small = (chunks, state, CHUNK)
    half = (chunks, state // 2, CHUNK)
    scratch = [
        pltpu.VMEM(small, F32), pltpu.VMEM(half, F32), pltpu.VMEM(half, F32),
        pltpu.VMEM(half, F32), pltpu.VMEM(half, F32),
        pltpu.VMEM(small, F32), pltpu.VMEM(half, F32), pltpu.VMEM(half, F32),
        pltpu.VMEM(half, F32), pltpu.VMEM(half, F32),
        pltpu.VMEM(small, F32), pltpu.VMEM(small, F32),
        pltpu.VMEM(half, F32), pltpu.VMEM(half, F32), pltpu.VMEM((chunks, CHUNK), F32),
        pltpu.VMEM((chunks, CHUNK), F32), pltpu.VMEM((chunks, CHUNK), F32),
        pltpu.VMEM(big, F32), pltpu.VMEM(big, F32), pltpu.VMEM(big, F32), pltpu.VMEM(big, F32),
        pltpu.VMEM(big, BF16),
        pltpu.VMEM((length, length), F32), pltpu.VMEM((length, length), F32),
        pltpu.VMEM((length, state), F32), pltpu.VMEM((length, state), F32),
        pltpu.VMEM((length, state), F32), pltpu.VMEM((128, length), F32), pltpu.VMEM((128, state), F32),
        pltpu.VMEM((8, 128), F32), pltpu.VMEM((n_dp - 1, 8, 128), F32),
    ]
    scratch += [pltpu.VMEM((8, 128), F32)] * 8
    scratch += [
        pltpu.VMEM((length, width), BF16), pltpu.VMEM((length, state), BF16),
        pltpu.VMEM((length, state), BF16), pltpu.VMEM((heads, length), F32),
        pltpu.VMEM((1, length), jnp.int32), pltpu.VMEM((1, length), F32),
        pltpu.VMEM((length, width), BF16), pltpu.SemaphoreType.DMA((7,)),
    ]
    scratch += [pltpu.SemaphoreType.DMA((chunks,))] * 17
    scratch += [pltpu.SemaphoreType.DMA((n_dp - 1,))] * 2
    scratch += [pltpu.SemaphoreType.DMA((5,))] * 2
    shapes = (
        ((length, width), BF16),
        ((length, width), BF16),
        ((length, state), BF16),
        ((length, state), BF16),
        ((heads, length), F32),
    )
    results = pl.pallas_call(
        functools.partial(kernel, n_seq, n_dp, heads),
        out_shape=tuple(pltpu.VMEM(*shape) for shape in shapes),
        in_specs=[pl.BlockSpec(memory_space=pltpu.HBM)] * 7,
        out_specs=(vmem,) * 5,
        scratch_shapes=scratch,
        compiler_params=pltpu.CompilerParams(
            collective_id=0, has_side_effects=True, vmem_limit_bytes=44 << 20
        ),
        name="mixing",
    )(
        *(
            pltpu.with_memory_space_constraint(x, pltpu.HBM)
            for x in (
                features[0], key_proj[0], query_proj[0], log_decay[0], doc_start, loss_weight,
                target[0],
            )
        )
    )
    stored = pl.pallas_call(
        store_kernel,
        out_shape=tuple(jax.ShapeDtypeStruct(*shape) for shape in shapes),
        in_specs=(vmem,) * 5,
        out_specs=(pl.BlockSpec(memory_space=pl.ANY),) * 5,
        scratch_shapes=[pltpu.SemaphoreType.DMA((5,))],
        name="store",
    )(*(pltpu.with_memory_space_constraint(r, pltpu.VMEM) for r in results))
    return tuple(r[None] for r in stored)


def solution(mesh):
    placed = (
        P("dp", "seq", None),
        P("dp", "seq", None),
        P("dp", "seq", None),
        P("dp", None, "seq"),
        P("dp", "seq"),
        P("dp", "seq"),
        P("dp", "seq", None),
    )
    return jax.shard_map(
        body,
        mesh=mesh,
        in_specs=placed,
        out_specs=(
            P("dp", "seq", None),
            P("dp", "seq", None),
            P("dp", "seq", None),
            P("dp", "seq", None),
            P("dp", None, "seq"),
        ),
        check_vma=False,
    )
```

```python
import functools
import math

import jax
import jax.numpy as jnp
from jax import lax
from jax.experimental import pallas as pl
from jax.experimental.pallas import tpu as pltpu
from jax.sharding import PartitionSpec as P

F32 = jnp.float32
BF16 = jnp.bfloat16
MESH = pl.DeviceIdType.MESH
CHUNK = 128
EARLY = 3
SUM_AT = 4
BEHIND = 4
RAW_F = ((9, 10), (9, 13), (1, 13))
RAW_B = ((0, 9), (2, 10), (0, 5))
DETOUR_F = ((7, 16), (5, 16), (6, 16))
DETOUR_B = ((0, 0), (0, 0), (0, 0))
LAG_DF = (7, 9, 4, 1)
LAG_DB = (2, 7, 2, 4)
LEAD = (11, 12, 14, 16)
LAG_Y = (15, 14, 10, 5)
LAG_Z = (28, 25, 20, 12)
LAG_B = (33, 34, 33, 20)


def mm(a, b):
    return jnp.dot(a, b, preferred_element_type=F32)


def mm_nt(a, b):
    return lax.dot_general(a, b, (((1,), (1,)), ((), ())), preferred_element_type=F32)


def split(x):
    hi = x.astype(BF16)
    lo = (x - hi.astype(F32)).astype(BF16)
    return hi, lo


def kernel(
    n_seq, n_dp, heads,
    f_hbm, k_hbm, q_hbm, ld_hbm, ds_hbm, w_hbm, t_hbm,
    out_ref, gf_ref, gk_ref, gq_ref, gd_ref,
    xf_send, xf_recv, zf_send, zf_recv, rf_send, xb_send, xb_recv, zb_send, zb_recv, rb_send,
    before_s, adjoint_s, raw_recv, via_recv, g_send, g_recv, g_diag,
    rise_s, inv_s, y_s, dl_s, lift_s,
    dmix_s, dmixt_s, dq_s, dk_s, gk_s, rt_s, ex_s,
    wown, wdp, wrow, wside, wpair, wup, wdown, wlow, whigh, om_s,
    f_ref, k_ref, q_ref, ld_ref, ds_ref, w_ref, t_ref, in_sem,
    xfs, xfr, zfs, zfr, rfs, rfr, xbs, xbr, zbs, zbr, rbs, rbr, rws, rwr, vis, vir, vos, wds, wdr, ones, oner,
):
    length, width = f_ref.shape
    state = k_ref.shape[1]
    head_size = width // heads
    chunks = width // CHUNK
    per_chunk = CHUNK // head_size
    sigma = 1.0 / math.sqrt(state * length)

    me = lax.axis_index("seq")
    row = lax.axis_index("dp")
    pair = me // 2
    pairs = n_seq // 2
    is_odd = me % 2
    odd = is_odd == 1
    partner = me + 1 - 2 * is_odd

    fetches = [
        pltpu.make_async_copy(src, dst, in_sem.at[i])
        for i, (src, dst) in enumerate(
            [
                (ld_hbm, ld_ref), (ds_hbm, ds_ref), (w_hbm, w_ref), (k_hbm, k_ref),
                (q_hbm, q_ref), (f_hbm, f_ref), (t_hbm, t_ref),
            ]
        )
    ]
    for fetch in fetches:
        fetch.start()
    barrier = pltpu.get_barrier_semaphore()

    def greet(target):
        pl.semaphore_signal(barrier, inc=1, device_id=target, device_id_type=MESH)

    def greet_dp(d, _):
        greet({"dp": (row + d) % n_dp})
        return 0

    has_low = pair > 0
    has_high = pair < pairs - 1
    greet({"seq": partner})

    @pl.when(has_low)
    def _():
        greet({"seq": me - 2})

    @pl.when(has_high)
    def _():
        greet({"seq": me + 2})

    even = is_odd == 0
    diag = me - 1 + 2 * is_odd
    has_diag = (odd & has_high) | (even & has_low)

    @pl.when(has_diag)
    def _():
        greet({"seq": diag})

    lax.fori_loop(1, n_dp, greet_dp, 0)
    greeters = n_dp + sum(flag.astype(jnp.int32) for flag in (has_low, has_high, has_diag))

    for fetch in fetches[:5]:
        fetch.wait()
    wown[...] = jnp.broadcast_to(jnp.sum(w_ref[...], axis=1, keepdims=True), wown.shape)

    starts = ds_ref[...].astype(F32)
    table = jnp.concatenate(
        [
            ld_ref[...],
            jnp.broadcast_to(starts, (8, length)),
            jnp.broadcast_to(w_ref[...], (8, length)),
            jnp.zeros((128 - heads - 16, length), F32),
        ],
        axis=0,
    )
    rows_i = lax.broadcasted_iota(jnp.int32, (length, length), 0)
    cols_i = lax.broadcasted_iota(jnp.int32, (length, length), 1)
    lower = (rows_i >= cols_i).astype(F32).astype(BF16)
    upper = (rows_i <= cols_i).astype(F32).astype(BF16)
    eye = (rows_i == cols_i).astype(F32).astype(BF16)
    eye_n = eye[:state, :state]
    table_hi, table_lo = split(table)
    cumulative = mm_nt(lower, table_hi) + mm_nt(lower, table_lo)
    turned = mm_nt(eye, table_hi) + mm_nt(eye, table_lo)
    seg_col = cumulative[:, heads:heads + 1]
    seg_row = mm(jnp.broadcast_to(starts, (8, length)).astype(BF16), upper)[0:1]
    last_seg = jnp.sum(starts, axis=1, keepdims=True)
    tail_row = (seg_row == last_seg).astype(F32)
    tail_col = (seg_col == last_seg).astype(F32)
    open_row = (seg_row == 0.0).astype(F32)
    open_col = (seg_col == 0.0).astype(F32)
    whole_block = (last_seg == 0.0).astype(F32)
    run_hi, run_lo = split(cumulative)

    keys = k_ref[...]
    queries = q_ref[...]
    keys_t = (mm_nt(eye_n, keys) * tail_row).astype(BF16)
    queries_t = (mm_nt(eye_n, queries) * open_row).astype(BF16)
    keys_tail = (keys.astype(F32) * tail_col).astype(BF16)
    queries_open = (queries.astype(F32) * open_col).astype(BF16)

    head_i = lax.broadcasted_iota(jnp.int32, (128, CHUNK), 0)
    lane_h = lax.broadcasted_iota(jnp.int32, (128, CHUNK), 1) // head_size

    def spread(c):
        return (head_i == lane_h + c * per_chunk).astype(F32).astype(BF16)

    def lanes(c):
        return pl.ds(pl.multiple_of(c * CHUNK, CHUNK), CHUNK)

    part = state // 2
    mine = pl.ds(pl.multiple_of(is_odd * part, part), part)
    theirs = pl.ds(pl.multiple_of((1 - is_odd) * part, part), part)

    def remote(src, dst, ss, rs, c, target):
        return pltpu.make_async_remote_copy(
            src_ref=src, dst_ref=dst, send_sem=ss.at[c], recv_sem=rs.at[c],
            device_id={"seq": target}, device_id_type=MESH,
        )

    def xf(c):
        return remote(xf_send.at[c, theirs], xf_recv.at[c], xfs, xfr, c, partner)

    def xb(c):
        return remote(xb_send.at[c, theirs], xb_recv.at[c], xbs, xbr, c, partner)

    def zf(c):
        return remote(zf_send.at[c], zf_recv.at[c], zfs, zfr, c, me + 2)

    def zb(c):
        return remote(zb_send.at[c], zb_recv.at[c], zbs, zbr, c, me - 2)

    def rf(c):
        return remote(rf_send.at[c], before_s.at[c, mine], rfs, rfr, c, partner)

    def rb(c):
        return remote(rb_send.at[c], adjoint_s.at[c, mine], rbs, rbr, c, partner)

    def single(src, dst, i, target):
        return pltpu.make_async_remote_copy(
            src_ref=src, dst_ref=dst, send_sem=ones.at[i], recv_sem=oner.at[i],
            device_id={"seq": target}, device_id_type=MESH,
        )

    def look_up(table, at, size, generic):
        if len(table) != size:
            return jnp.int32(generic)
        found = jnp.int32(0)
        for i, n in enumerate(table):
            found = jnp.where(at == i, n * chunks // 16, found)
        return found

    def raw(src, c):
        return remote(src.at[c, theirs], raw_recv.at[c], rws, rwr, c, diag)

    def via(src, c):
        return remote(src.at[c], via_recv.at[c], vis, vir, c, partner)

    def on_f(c):
        return remote(via_recv.at[c], before_s.at[c, theirs], vos, rfr, c, me + 2)

    def on_b(c):
        return remote(via_recv.at[c], adjoint_s.at[c, theirs], vos, rbr, c, me - 2)

    def within(c, table, at):
        inside = c < 0
        if len(table) == pairs - 1:
            for i, (low, high) in enumerate(table):
                if low < high:
                    inside = inside | (
                        (at == i) & (c >= low * chunks // 16) & (c < high * chunks // 16)
                    )
        return inside

    def raw_f_out(c):
        return odd & within(c, RAW_F, pair)

    def raw_f_pass(c):
        return even & within(c, RAW_F, pair)

    def raw_f_in(c):
        return even & within(c, RAW_F, pair - 1)

    def raw_b_out(c):
        return even & within(c, RAW_B, pair - 1)

    def raw_b_pass(c):
        return odd & within(c, RAW_B, pair - 1)

    def raw_b_in(c):
        return odd & within(c, RAW_B, pair)

    def via_f_out(c):
        return odd & within(c, DETOUR_F, pair)

    def via_f_on(c):
        return even & within(c, DETOUR_F, pair)

    def via_f_skip(c):
        return odd & within(c, DETOUR_F, pair - 1)

    def via_b_out(c):
        return even & within(c, DETOUR_B, pair - 1)

    def via_b_on(c):
        return odd & within(c, DETOUR_B, pair - 1)

    def via_b_skip(c):
        return even & within(c, DETOUR_B, pair)

    to_next = even | has_high
    from_next = odd | has_high
    to_last = odd | has_low
    from_last = even | has_low

    def w_dp(d):
        return pltpu.make_async_remote_copy(
            src_ref=wrow, dst_ref=wdp.at[d - 1], send_sem=wds.at[d - 1], recv_sem=wdr.at[d - 1],
            device_id={"dp": (row + d) % n_dp}, device_id_type=MESH,
        )

    chunk_i = lax.broadcasted_iota(jnp.int32, (chunks, 128), 0)
    of_chunk = lax.broadcasted_iota(jnp.int32, (chunks, 128), 1) // per_chunk
    of_lane = (head_i % per_chunk == lane_h).astype(F32).astype(BF16)

    def pick(part):
        last = jnp.broadcast_to(part[length - 1:length].astype(F32), (chunks, 128))
        return mm(jnp.where(of_chunk == chunk_i, last, 0.0).astype(BF16), of_lane)

    g_send[...] = jnp.exp(pick(run_hi) + pick(run_lo)) * whole_block

    def fresh_step(c, _):
        e = spread(c)
        run_x = mm(run_hi, e) + mm(run_lo, e)
        rise = jnp.exp(run_x)
        inv = jnp.exp(-run_x)
        lifted = (f_ref[:, lanes(c)].astype(F32) * inv).astype(BF16)
        xf_send[c] = mm(keys_t, lifted) * (rise[length - 1:length] * sigma)
        rise_s[c] = rise
        inv_s[c] = inv
        lift_s[c] = lifted
        return 0

    def send_fresh(c, _):
        @pl.when(to_next & ~raw_f_out(c))
        def _():
            xf(c).start()

        @pl.when(raw_f_out(c))
        def _():
            raw(xf_send, c).start()

        return 0

    def fresh_and_send(c, _):
        fresh_step(c, 0)
        send_fresh(c, 0)
        return 0

    def start_w(d, _):
        w_dp(d).start()
        return 0

    linked = (rows_i >= cols_i) & (seg_col == seg_row)
    linked_t = (rows_i <= cols_i) & (seg_col == seg_row)
    fetches[5].wait()
    first = min(EARLY, chunks)
    lax.fori_loop(0, first, fresh_step, 0)
    @pl.when(pair == 0)
    def _():
        zf_recv[...] = jnp.zeros_like(zf_recv)
        wlow[...] = jnp.zeros_like(wlow)

        @pl.when(even)
        def _():
            before_s[...] = jnp.zeros_like(before_s)

    @pl.when(pair == pairs - 1)
    def _():
        zb_recv[...] = jnp.zeros_like(zb_recv)
        whigh[...] = jnp.zeros_like(whigh)

        @pl.when(odd)
        def _():
            adjoint_s[...] = jnp.zeros_like(adjoint_s)

    lead = jnp.maximum(first, look_up(LEAD, pair, pairs, chunks))
    lag_y = look_up(LAG_Y, pair, pairs, 0)
    sum_at = min(SUM_AT, chunks - 1)
    generic_lag = jnp.minimum(chunks, 3 + 5 * (pairs - 1 - pair))
    lag_z = jnp.maximum(look_up(LAG_Z, pair, pairs, generic_lag), jnp.maximum(lag_y, sum_at))
    lag_v = lag_z + look_up(LAG_DB, pair, pairs, 0)
    lag_u = look_up(LAG_DF, pair, pairs, 0)
    lag_b = jnp.maximum(look_up(LAG_B, pair, pairs, generic_lag), lag_v)

    pl.semaphore_wait(barrier, greeters)
    single(g_send, g_recv, 0, partner).start()
    single(wown, wside, 1, partner).start()

    @pl.when(has_diag)
    def _():
        single(g_send, g_diag, 4, diag).start()

    lax.fori_loop(0, first, send_fresh, 0)
    mixing = jnp.where(linked, mm_nt(queries, keys) * sigma, 0.0).astype(BF16)
    mixing_t = jnp.where(linked_t, mm_nt(keys, queries) * sigma, 0.0).astype(BF16)
    dmix_s[...] = jnp.zeros_like(dmix_s)
    dmixt_s[...] = jnp.zeros_like(dmixt_s)
    dq_s[...] = jnp.zeros_like(dq_s)
    dk_s[...] = jnp.zeros_like(dk_s)
    rt_s[...] = jnp.zeros_like(rt_s)
    ex_s[...] = jnp.zeros_like(ex_s)

    lax.fori_loop(first, lead, fresh_and_send, 0)
    single(wown, wside, 1, partner).wait_recv()
    wrow[...] = wown[...] + wside[...]
    lax.fori_loop(1, n_dp, start_w, 0)
    single(g_send, g_recv, 0, partner).wait_recv()

    @pl.when(has_diag)
    def _():
        single(g_send, g_diag, 4, diag).wait_recv()

    fetches[6].wait()
    weight = turned[:, heads + 8:heads + 9]

    def add_w(d, total):
        w_dp(d).wait_recv()
        return total + wdp[d - 1]

    def carry_forward(c):
        @pl.when(c == sum_at)
        def _():
            wpair[...] = lax.fori_loop(1, n_dp, add_w, wrow[...])

            @pl.when(has_low)
            def _():
                single(wup, wlow, 2, me).wait_recv()

            wup[...] = wlow[...] + wpair[...]

            @pl.when(has_high)
            def _():
                single(wup, wlow, 2, me + 2).start()

        @pl.when(has_low)
        def _():
            zf(c).wait_recv()

        @pl.when(from_next & ~raw_f_pass(c))
        def _():
            xf(c).wait_recv()

        @pl.when(raw_f_in(c))
        def _():
            raw(xf_send, c).wait_recv()

        own_keep = g_send[pl.ds(c, 1), :]
        other_keep = g_recv[pl.ds(c, 1), :]
        own = xf_send[c, mine]
        other = xf_recv[c]
        carried = zf_recv[c]
        diag_keep = g_diag[pl.ds(c, 1), :]
        entry = jnp.where(raw_f_in(c), raw_recv[c] + diag_keep * carried, carried)
        middle = jnp.where(odd, other, own) + jnp.where(odd, other_keep, own_keep) * entry
        onward = jnp.where(odd, own, other) + jnp.where(odd, own_keep, other_keep) * middle
        zf_send[c] = jnp.where(raw_f_pass(c), middle, onward)

        @pl.when(has_high)
        def _():
            zf(c).start()

        rf_send[c] = jnp.where(odd, entry, middle)

        @pl.when(from_last & ~via_f_skip(c))
        def _():
            rf(c).start()

        @pl.when(via_f_out(c))
        def _():
            via(zf_send, c).start()

        before_s[c, mine] = jnp.where(odd, middle, entry)

    def pass_forward(c):
        @pl.when(via_f_on(c))
        def _():
            via(zf_send, c).wait_recv()
            on_f(c).start()

    def pass_backward(c):
        @pl.when(via_b_on(c))
        def _():
            via(zb_send, c).wait_recv()
            on_b(c).start()

    def forward_step(c):
        @pl.when(to_last)
        def _():
            rf(c).wait_recv()

        before_h = before_s[c].astype(BF16)
        rise = rise_s[c]
        lifted = lift_s[c]
        y = rise * (mm(mixing, lifted) + mm(queries_open, before_h))
        grad = weight * (y - t_ref[:, lanes(c)].astype(F32))
        z = (grad * rise).astype(BF16)
        xb_send[c] = mm(queries_t, z)

        @pl.when(to_last & ~raw_b_out(c))
        def _():
            xb(c).start()

        @pl.when(raw_b_out(c))
        def _():
            raw(xb_send, c).start()

        out_ref[:, lanes(c)] = y.astype(BF16)
        y_s[c] = grad * y
        dq_s[...] += mm_nt(z, before_h)
        dmix_s[...] += mm_nt(z, lifted)
        dmixt_s[...] += mm_nt(lifted, z)
        dl_s[c] = mm(mixing_t, z)

    def sent_forward(c):
        @pl.when(to_next & ~raw_f_out(c))
        def _():
            xf(c).wait_send()

        @pl.when(raw_f_out(c))
        def _():
            raw(xf_send, c).wait_send()

        @pl.when(from_last & ~via_f_skip(c))
        def _():
            rf(c).wait_send()

        @pl.when(via_f_out(c))
        def _():
            via(zf_send, c).wait_send()

        @pl.when(via_f_on(c))
        def _():
            on_f(c).wait_send()

        @pl.when(has_high)
        def _():
            zf(c).wait_send()

    def sent_backward(c):
        @pl.when(to_last & ~raw_b_out(c))
        def _():
            xb(c).wait_send()

        @pl.when(raw_b_out(c))
        def _():
            raw(xb_send, c).wait_send()

        @pl.when(from_next & ~via_b_skip(c))
        def _():
            rb(c).wait_send()

        @pl.when(via_b_out(c))
        def _():
            via(zb_send, c).wait_send()

        @pl.when(via_b_on(c))
        def _():
            on_b(c).wait_send()

        @pl.when(has_low)
        def _():
            zb(c).wait_send()

    def carry_backward(c):
        @pl.when(has_high)
        def _():
            zb(c).wait_recv()

        @pl.when(from_last & ~raw_b_pass(c))
        def _():
            xb(c).wait_recv()

        @pl.when(raw_b_in(c))
        def _():
            raw(xb_send, c).wait_recv()

        own_keep = g_send[pl.ds(c, 1), :]
        other_keep = g_recv[pl.ds(c, 1), :]
        own = xb_send[c, mine]
        other = xb_recv[c]
        carried = zb_recv[c]
        diag_keep = g_diag[pl.ds(c, 1), :]
        entry = jnp.where(raw_b_in(c), raw_recv[c] + diag_keep * carried, carried)
        middle = jnp.where(odd, own, other) + jnp.where(odd, own_keep, other_keep) * entry
        onward = jnp.where(odd, other, own) + jnp.where(odd, other_keep, own_keep) * middle
        zb_send[c] = jnp.where(raw_b_pass(c), middle, onward)

        @pl.when(has_low)
        def _():
            zb(c).start()

        rb_send[c] = jnp.where(odd, middle, entry)

        @pl.when(from_next & ~via_b_skip(c))
        def _():
            rb(c).start()

        @pl.when(via_b_out(c))
        def _():
            via(zb_send, c).start()

        adjoint_s[c, mine] = jnp.where(odd, entry, middle)

        @pl.when(c == 0)
        def _():
            @pl.when(has_high)
            def _():
                single(wdown, whigh, 3, me).wait_recv()

            wdown[...] = whigh[...] + wpair[...]

            @pl.when(has_low)
            def _():
                single(wdown, whigh, 3, me - 2).start()

            om_s[...] = (length * n_seq * n_dp) / (wlow[...] + wpair[...] + whigh[...])

    def backward_step(c):
        @pl.when(to_next)
        def _():
            rb(c).wait_recv()

        over_mean = om_s[0:1, 0:1]
        e = spread(c)
        gain = rise_s[c, length - 1:length, :]
        adjoint = adjoint_s[c] * over_mean
        scaled = (adjoint * (gain * sigma)).astype(BF16)
        d_feature = inv_s[c] * (dl_s[c] * over_mean + mm(keys_tail, scaled))
        gf_ref[:, lanes(c)] = d_feature.astype(BF16)
        change = y_s[c] * over_mean - f_ref[:, lanes(c)].astype(F32) * d_feature
        change_hi, change_lo = split(change)
        rt_s[...] += mm_nt(e, change_hi) + mm_nt(e, change_lo)
        dk_s[...] += mm_nt(lift_s[c], scaled)
        after = xf_send[c] + g_send[pl.ds(c, 1), :] * before_s[c]
        end_hi, end_lo = split(adjoint * after)
        ex_s[...] += mm_nt(e, end_hi) + mm_nt(e, end_lo)
        sent_forward(c)

        @pl.when(c >= BEHIND)
        def _():
            sent_backward(c - BEHIND)

    def finish_scores():
        over_mean = om_s[0:1, 0:1]
        d_scores = (jnp.where(linked, dmix_s[...], 0.0) * (over_mean * sigma)).astype(BF16)
        d_scores_t = (jnp.where(linked_t, dmixt_s[...], 0.0) * (over_mean * sigma)).astype(BF16)
        gq_ref[...] = (mm(d_scores, keys) + (open_col * over_mean) * dq_s[...]).astype(BF16)
        gk_s[...] = mm(d_scores_t, queries)

    def step(i, _):
        @pl.when(i + lead < chunks)
        def _():
            fresh_and_send(i + lead, 0)

        @pl.when(i < chunks)
        def _():
            carry_forward(i)

        @pl.when((i >= lag_u) & (i < lag_u + chunks))
        def _():
            pass_forward(i - lag_u)

        @pl.when((i >= lag_y) & (i < lag_y + chunks))
        def _():
            forward_step(i - lag_y)

        @pl.when((i >= lag_z) & (i < lag_z + chunks))
        def _():
            carry_backward(i - lag_z)

        @pl.when((i >= lag_v) & (i < lag_v + chunks))
        def _():
            pass_backward(i - lag_v)

        @pl.when(i == jnp.maximum(chunks + lag_y, lag_z + 1))
        def _():
            finish_scores()

        @pl.when((i >= lag_b) & (i < lag_b + chunks))
        def _():
            backward_step(i - lag_b)

        return 0

    end = jnp.maximum(chunks + jnp.maximum(lag_b, jnp.maximum(lag_y + 1, lag_u)), lag_z + 2)
    lax.fori_loop(0, end, step, 0)

    gk_ref[...] = (gk_s[...] + tail_col * dk_s[...]).astype(BF16)
    rt_hi, rt_lo = split(rt_s[...])
    decay = mm(rt_hi, lower) + mm(rt_lo, lower) + jnp.sum(ex_s[...], axis=1, keepdims=True)
    gd_ref[...] = decay[:heads]

    def finish_step(c, _):
        sent_backward(c)
        return 0

    lax.fori_loop(max(chunks - BEHIND, 0), chunks, finish_step, 0)

    def finish_w(d, _):
        w_dp(d).wait_send()
        return 0

    lax.fori_loop(1, n_dp, finish_w, 0)
    single(g_send, g_recv, 0, partner).wait_send()

    @pl.when(has_diag)
    def _():
        single(g_send, g_diag, 4, diag).wait_send()
    single(wown, wside, 1, partner).wait_send()

    @pl.when(has_high)
    def _():
        single(wup, wlow, 2, me + 2).wait_send()

    @pl.when(has_low)
    def _():
        single(wdown, whigh, 3, me - 2).wait_send()


def store_kernel(*refs):
    count = len(refs) // 2
    sem = refs[-1]
    copies = [
        pltpu.make_async_copy(refs[i], refs[count + i], sem.at[i]) for i in range(count)
    ]
    for copy in copies:
        copy.start()
    for copy in copies:
        copy.wait()


def body(features, key_proj, query_proj, log_decay, doc_start, loss_weight, target):
    n_seq, n_dp = lax.axis_size("seq"), lax.axis_size("dp")
    length, width = features.shape[1:]
    state = key_proj.shape[2]
    heads = log_decay.shape[1]
    chunks = width // CHUNK
    vmem = pl.BlockSpec(memory_space=pltpu.VMEM)
    big = (chunks, length, CHUNK)
    small = (chunks, state, CHUNK)
    half = (chunks, state // 2, CHUNK)
    scratch = [
        pltpu.VMEM(small, F32), pltpu.VMEM(half, F32), pltpu.VMEM(half, F32),
        pltpu.VMEM(half, F32), pltpu.VMEM(half, F32),
        pltpu.VMEM(small, F32), pltpu.VMEM(half, F32), pltpu.VMEM(half, F32),
        pltpu.VMEM(half, F32), pltpu.VMEM(half, F32),
        pltpu.VMEM(small, F32), pltpu.VMEM(small, F32),
        pltpu.VMEM(half, F32), pltpu.VMEM(half, F32), pltpu.VMEM((chunks, CHUNK), F32),
        pltpu.VMEM((chunks, CHUNK), F32), pltpu.VMEM((chunks, CHUNK), F32),
        pltpu.VMEM(big, F32), pltpu.VMEM(big, F32), pltpu.VMEM(big, F32), pltpu.VMEM(big, F32),
        pltpu.VMEM(big, BF16),
        pltpu.VMEM((length, length), F32), pltpu.VMEM((length, length), F32),
        pltpu.VMEM((length, state), F32), pltpu.VMEM((length, state), F32),
        pltpu.VMEM((length, state), F32), pltpu.VMEM((128, length), F32), pltpu.VMEM((128, state), F32),
        pltpu.VMEM((8, 128), F32), pltpu.VMEM((n_dp - 1, 8, 128), F32),
    ]
    scratch += [pltpu.VMEM((8, 128), F32)] * 8
    scratch += [
        pltpu.VMEM((length, width), BF16), pltpu.VMEM((length, state), BF16),
        pltpu.VMEM((length, state), BF16), pltpu.VMEM((heads, length), F32),
        pltpu.VMEM((1, length), jnp.int32), pltpu.VMEM((1, length), F32),
        pltpu.VMEM((length, width), BF16), pltpu.SemaphoreType.DMA((7,)),
    ]
    scratch += [pltpu.SemaphoreType.DMA((chunks,))] * 17
    scratch += [pltpu.SemaphoreType.DMA((n_dp - 1,))] * 2
    scratch += [pltpu.SemaphoreType.DMA((5,))] * 2
    shapes = (
        ((length, width), BF16),
        ((length, width), BF16),
        ((length, state), BF16),
        ((length, state), BF16),
        ((heads, length), F32),
    )
    results = pl.pallas_call(
        functools.partial(kernel, n_seq, n_dp, heads),
        out_shape=tuple(pltpu.VMEM(*shape) for shape in shapes),
        in_specs=[pl.BlockSpec(memory_space=pltpu.HBM)] * 7,
        out_specs=(vmem,) * 5,
        scratch_shapes=scratch,
        compiler_params=pltpu.CompilerParams(
            collective_id=0, has_side_effects=True, vmem_limit_bytes=44 << 20
        ),
        name="mixing",
    )(
        *(
            pltpu.with_memory_space_constraint(x, pltpu.HBM)
            for x in (
                features[0], key_proj[0], query_proj[0], log_decay[0], doc_start, loss_weight,
                target[0],
            )
        )
    )
    stored = pl.pallas_call(
        store_kernel,
        out_shape=tuple(jax.ShapeDtypeStruct(*shape) for shape in shapes),
        in_specs=(vmem,) * 5,
        out_specs=(pl.BlockSpec(memory_space=pl.ANY),) * 5,
        scratch_shapes=[pltpu.SemaphoreType.DMA((5,))],
        name="store",
    )(*(pltpu.with_memory_space_constraint(r, pltpu.VMEM) for r in results))
    return tuple(r[None] for r in stored)


def solution(mesh):
    placed = (
        P("dp", "seq", None),
        P("dp", "seq", None),
        P("dp", "seq", None),
        P("dp", None, "seq"),
        P("dp", "seq"),
        P("dp", "seq"),
        P("dp", "seq", None),
    )
    return jax.shard_map(
        body,
        mesh=mesh,
        in_specs=placed,
        out_specs=(
            P("dp", "seq", None),
            P("dp", "seq", None),
            P("dp", "seq", None),
            P("dp", "seq", None),
            P("dp", None, "seq"),
        ),
        check_vma=False,
    )
```

```python
import functools
import math

import jax
import jax.numpy as jnp
from jax import lax
from jax.experimental import pallas as pl
from jax.experimental.pallas import tpu as pltpu
from jax.sharding import PartitionSpec as P

F32 = jnp.float32
BF16 = jnp.bfloat16
MESH = pl.DeviceIdType.MESH
CHUNK = 128
EARLY = 2
SUM_AT = 4
BEHIND = 4
RAW_F = ((9, 10), (9, 13), (1, 13))
RAW_B = ((0, 9), (2, 10), (0, 5))
DETOUR_F = ((7, 16), (5, 16), (6, 16))
DETOUR_B = ((0, 0), (0, 0), (0, 0))
LAG_DF = (7, 9, 4, 1)
LAG_DB = (2, 7, 2, 4)
LEAD = (11, 12, 14, 16)
LAG_Y = (15, 14, 10, 5)
LAG_Z = (28, 25, 20, 12)
LAG_B = (33, 34, 33, 20)


def mm(a, b):
    return jnp.dot(a, b, preferred_element_type=F32)


def mm_nt(a, b):
    return lax.dot_general(a, b, (((1,), (1,)), ((), ())), preferred_element_type=F32)


def split(x):
    hi = x.astype(BF16)
    lo = (x - hi.astype(F32)).astype(BF16)
    return hi, lo


def kernel(
    n_seq, n_dp, heads,
    f_hbm, k_hbm, q_hbm, ld_hbm, ds_hbm, w_hbm, t_hbm,
    out_ref, gf_ref, gk_ref, gq_ref, gd_ref,
    xf_send, xf_recv, zf_send, zf_recv, rf_send, xb_send, xb_recv, zb_send, zb_recv, rb_send,
    before_s, adjoint_s, raw_recv, via_recv, g_send, g_recv, g_diag,
    rise_s, inv_s, y_s, dl_s, lift_s,
    dmix_s, dmixt_s, dq_s, dk_s, gk_s, rt_s, ex_s,
    wown, wdp, wrow, wside, wpair, wup, wdown, wlow, whigh, om_s,
    f_ref, k_ref, q_ref, ld_ref, ds_ref, w_ref, t_ref, in_sem,
    xfs, xfr, zfs, zfr, rfs, rfr, xbs, xbr, zbs, zbr, rbs, rbr, rws, rwr, vis, vir, vos, wds, wdr, ones, oner,
):
    length, width = f_ref.shape
    state = k_ref.shape[1]
    head_size = width // heads
    chunks = width // CHUNK
    per_chunk = CHUNK // head_size
    sigma = 1.0 / math.sqrt(state * length)

    me = lax.axis_index("seq")
    row = lax.axis_index("dp")
    pair = me // 2
    pairs = n_seq // 2
    is_odd = me % 2
    odd = is_odd == 1
    partner = me + 1 - 2 * is_odd

    fetches = [
        pltpu.make_async_copy(src, dst, in_sem.at[i])
        for i, (src, dst) in enumerate(
            [
                (ld_hbm, ld_ref), (ds_hbm, ds_ref), (w_hbm, w_ref), (k_hbm, k_ref),
                (q_hbm, q_ref), (f_hbm, f_ref), (t_hbm, t_ref),
            ]
        )
    ]
    for fetch in fetches:
        fetch.start()
    barrier = pltpu.get_barrier_semaphore()

    def greet(target):
        pl.semaphore_signal(barrier, inc=1, device_id=target, device_id_type=MESH)

    def greet_dp(d, _):
        greet({"dp": (row + d) % n_dp})
        return 0

    has_low = pair > 0
    has_high = pair < pairs - 1
    greet({"seq": partner})

    @pl.when(has_low)
    def _():
        greet({"seq": me - 2})

    @pl.when(has_high)
    def _():
        greet({"seq": me + 2})

    even = is_odd == 0
    diag = me - 1 + 2 * is_odd
    has_diag = (odd & has_high) | (even & has_low)

    @pl.when(has_diag)
    def _():
        greet({"seq": diag})

    lax.fori_loop(1, n_dp, greet_dp, 0)
    greeters = n_dp + sum(flag.astype(jnp.int32) for flag in (has_low, has_high, has_diag))

    for fetch in fetches[:5]:
        fetch.wait()
    wown[...] = jnp.broadcast_to(jnp.sum(w_ref[...], axis=1, keepdims=True), wown.shape)

    starts = ds_ref[...].astype(F32)
    table = jnp.concatenate(
        [
            ld_ref[...],
            jnp.broadcast_to(starts, (8, length)),
            jnp.broadcast_to(w_ref[...], (8, length)),
            jnp.zeros((128 - heads - 16, length), F32),
        ],
        axis=0,
    )
    rows_i = lax.broadcasted_iota(jnp.int32, (length, length), 0)
    cols_i = lax.broadcasted_iota(jnp.int32, (length, length), 1)
    lower = (rows_i >= cols_i).astype(F32).astype(BF16)
    upper = (rows_i <= cols_i).astype(F32).astype(BF16)
    eye = (rows_i == cols_i).astype(F32).astype(BF16)
    eye_n = eye[:state, :state]
    table_hi, table_lo = split(table)
    cumulative = mm_nt(lower, table_hi) + mm_nt(lower, table_lo)
    turned = mm_nt(eye, table_hi) + mm_nt(eye, table_lo)
    seg_col = cumulative[:, heads:heads + 1]
    seg_row = mm(jnp.broadcast_to(starts, (8, length)).astype(BF16), upper)[0:1]
    last_seg = jnp.sum(starts, axis=1, keepdims=True)
    tail_row = (seg_row == last_seg).astype(F32)
    tail_col = (seg_col == last_seg).astype(F32)
    open_row = (seg_row == 0.0).astype(F32)
    open_col = (seg_col == 0.0).astype(F32)
    whole_block = (last_seg == 0.0).astype(F32)
    run_hi, run_lo = split(cumulative)

    keys = k_ref[...]
    queries = q_ref[...]
    keys_t = (mm_nt(eye_n, keys) * tail_row).astype(BF16)
    queries_t = (mm_nt(eye_n, queries) * open_row).astype(BF16)
    keys_tail = (keys.astype(F32) * tail_col).astype(BF16)
    queries_open = (queries.astype(F32) * open_col).astype(BF16)

    head_i = lax.broadcasted_iota(jnp.int32, (128, CHUNK), 0)
    lane_h = lax.broadcasted_iota(jnp.int32, (128, CHUNK), 1) // head_size

    def spread(c):
        return (head_i == lane_h + c * per_chunk).astype(F32).astype(BF16)

    def lanes(c):
        return pl.ds(pl.multiple_of(c * CHUNK, CHUNK), CHUNK)

    part = state // 2
    mine = pl.ds(pl.multiple_of(is_odd * part, part), part)
    theirs = pl.ds(pl.multiple_of((1 - is_odd) * part, part), part)

    def remote(src, dst, ss, rs, c, target):
        return pltpu.make_async_remote_copy(
            src_ref=src, dst_ref=dst, send_sem=ss.at[c], recv_sem=rs.at[c],
            device_id={"seq": target}, device_id_type=MESH,
        )

    def xf(c):
        return remote(xf_send.at[c, theirs], xf_recv.at[c], xfs, xfr, c, partner)

    def xb(c):
        return remote(xb_send.at[c, theirs], xb_recv.at[c], xbs, xbr, c, partner)

    def zf(c):
        return remote(zf_send.at[c], zf_recv.at[c], zfs, zfr, c, me + 2)

    def zb(c):
        return remote(zb_send.at[c], zb_recv.at[c], zbs, zbr, c, me - 2)

    def rf(c):
        return remote(rf_send.at[c], before_s.at[c, mine], rfs, rfr, c, partner)

    def rb(c):
        return remote(rb_send.at[c], adjoint_s.at[c, mine], rbs, rbr, c, partner)

    def single(src, dst, i, target):
        return pltpu.make_async_remote_copy(
            src_ref=src, dst_ref=dst, send_sem=ones.at[i], recv_sem=oner.at[i],
            device_id={"seq": target}, device_id_type=MESH,
        )

    def look_up(table, at, size, generic):
        if len(table) != size:
            return jnp.int32(generic)
        found = jnp.int32(0)
        for i, n in enumerate(table):
            found = jnp.where(at == i, n * chunks // 16, found)
        return found

    def raw(src, c):
        return remote(src.at[c, theirs], raw_recv.at[c], rws, rwr, c, diag)

    def via(src, c):
        return remote(src.at[c], via_recv.at[c], vis, vir, c, partner)

    def on_f(c):
        return remote(via_recv.at[c], before_s.at[c, theirs], vos, rfr, c, me + 2)

    def on_b(c):
        return remote(via_recv.at[c], adjoint_s.at[c, theirs], vos, rbr, c, me - 2)

    def within(c, table, at):
        inside = c < 0
        if len(table) == pairs - 1:
            for i, (low, high) in enumerate(table):
                if low < high:
                    inside = inside | (
                        (at == i) & (c >= low * chunks // 16) & (c < high * chunks // 16)
                    )
        return inside

    def raw_f_out(c):
        return odd & within(c, RAW_F, pair)

    def raw_f_pass(c):
        return even & within(c, RAW_F, pair)

    def raw_f_in(c):
        return even & within(c, RAW_F, pair - 1)

    def raw_b_out(c):
        return even & within(c, RAW_B, pair - 1)

    def raw_b_pass(c):
        return odd & within(c, RAW_B, pair - 1)

    def raw_b_in(c):
        return odd & within(c, RAW_B, pair)

    def via_f_out(c):
        return odd & within(c, DETOUR_F, pair)

    def via_f_on(c):
        return even & within(c, DETOUR_F, pair)

    def via_f_skip(c):
        return odd & within(c, DETOUR_F, pair - 1)

    def via_b_out(c):
        return even & within(c, DETOUR_B, pair - 1)

    def via_b_on(c):
        return odd & within(c, DETOUR_B, pair - 1)

    def via_b_skip(c):
        return even & within(c, DETOUR_B, pair)

    to_next = even | has_high
    from_next = odd | has_high
    to_last = odd | has_low
    from_last = even | has_low

    def w_dp(d):
        return pltpu.make_async_remote_copy(
            src_ref=wrow, dst_ref=wdp.at[d - 1], send_sem=wds.at[d - 1], recv_sem=wdr.at[d - 1],
            device_id={"dp": (row + d) % n_dp}, device_id_type=MESH,
        )

    chunk_i = lax.broadcasted_iota(jnp.int32, (chunks, 128), 0)
    of_chunk = lax.broadcasted_iota(jnp.int32, (chunks, 128), 1) // per_chunk
    of_lane = (head_i % per_chunk == lane_h).astype(F32).astype(BF16)

    def pick(part):
        last = jnp.broadcast_to(part[length - 1:length].astype(F32), (chunks, 128))
        return mm(jnp.where(of_chunk == chunk_i, last, 0.0).astype(BF16), of_lane)

    g_send[...] = jnp.exp(pick(run_hi) + pick(run_lo)) * whole_block

    def fresh_step(c, _):
        e = spread(c)
        run_x = mm(run_hi, e) + mm(run_lo, e)
        rise = jnp.exp(run_x)
        inv = jnp.exp(-run_x)
        lifted = (f_ref[:, lanes(c)].astype(F32) * inv).astype(BF16)
        xf_send[c] = mm(keys_t, lifted) * (rise[length - 1:length] * sigma)
        rise_s[c] = rise
        inv_s[c] = inv
        lift_s[c] = lifted
        return 0

    def send_fresh(c, _):
        @pl.when(to_next & ~raw_f_out(c))
        def _():
            xf(c).start()

        @pl.when(raw_f_out(c))
        def _():
            raw(xf_send, c).start()

        return 0

    def fresh_and_send(c, _):
        fresh_step(c, 0)
        send_fresh(c, 0)
        return 0

    def start_w(d, _):
        w_dp(d).start()
        return 0

    linked = (rows_i >= cols_i) & (seg_col == seg_row)
    linked_t = (rows_i <= cols_i) & (seg_col == seg_row)
    fetches[5].wait()
    first = min(EARLY, chunks)
    lax.fori_loop(0, first, fresh_step, 0)
    lead = jnp.maximum(first, look_up(LEAD, pair, pairs, chunks))
    lag_y = look_up(LAG_Y, pair, pairs, 0)
    sum_at = min(SUM_AT, chunks - 1)
    generic_lag = jnp.minimum(chunks, 3 + 5 * (pairs - 1 - pair))
    lag_z = jnp.maximum(look_up(LAG_Z, pair, pairs, generic_lag), jnp.maximum(lag_y, sum_at))
    lag_v = lag_z + look_up(LAG_DB, pair, pairs, 0)
    lag_u = look_up(LAG_DF, pair, pairs, 0)
    lag_b = jnp.maximum(look_up(LAG_B, pair, pairs, generic_lag), lag_v)

    pl.semaphore_wait(barrier, greeters)
    single(g_send, g_recv, 0, partner).start()
    single(wown, wside, 1, partner).start()

    @pl.when(has_diag)
    def _():
        single(g_send, g_diag, 4, diag).start()

    lax.fori_loop(0, first, send_fresh, 0)

    @pl.when(pair == 0)
    def _():
        zf_recv[...] = jnp.zeros_like(zf_recv)
        wlow[...] = jnp.zeros_like(wlow)

        @pl.when(even)
        def _():
            before_s[...] = jnp.zeros_like(before_s)

    @pl.when(pair == pairs - 1)
    def _():
        zb_recv[...] = jnp.zeros_like(zb_recv)
        whigh[...] = jnp.zeros_like(whigh)

        @pl.when(odd)
        def _():
            adjoint_s[...] = jnp.zeros_like(adjoint_s)

    mixing = jnp.where(linked, mm_nt(queries, keys) * sigma, 0.0).astype(BF16)
    mixing_t = jnp.where(linked_t, mm_nt(keys, queries) * sigma, 0.0).astype(BF16)
    dmix_s[...] = jnp.zeros_like(dmix_s)
    dmixt_s[...] = jnp.zeros_like(dmixt_s)
    dq_s[...] = jnp.zeros_like(dq_s)
    dk_s[...] = jnp.zeros_like(dk_s)
    rt_s[...] = jnp.zeros_like(rt_s)
    ex_s[...] = jnp.zeros_like(ex_s)

    lax.fori_loop(first, lead, fresh_and_send, 0)
    single(wown, wside, 1, partner).wait_recv()
    wrow[...] = wown[...] + wside[...]
    lax.fori_loop(1, n_dp, start_w, 0)
    single(g_send, g_recv, 0, partner).wait_recv()

    @pl.when(has_diag)
    def _():
        single(g_send, g_diag, 4, diag).wait_recv()

    fetches[6].wait()
    weight = turned[:, heads + 8:heads + 9]

    def add_w(d, total):
        w_dp(d).wait_recv()
        return total + wdp[d - 1]

    def carry_forward(c):
        @pl.when(c == sum_at)
        def _():
            wpair[...] = lax.fori_loop(1, n_dp, add_w, wrow[...])

            @pl.when(has_low)
            def _():
                single(wup, wlow, 2, me).wait_recv()

            wup[...] = wlow[...] + wpair[...]

            @pl.when(has_high)
            def _():
                single(wup, wlow, 2, me + 2).start()

        @pl.when(has_low)
        def _():
            zf(c).wait_recv()

        @pl.when(from_next & ~raw_f_pass(c))
        def _():
            xf(c).wait_recv()

        @pl.when(raw_f_in(c))
        def _():
            raw(xf_send, c).wait_recv()

        own_keep = g_send[pl.ds(c, 1), :]
        other_keep = g_recv[pl.ds(c, 1), :]
        own = xf_send[c, mine]
        other = xf_recv[c]
        carried = zf_recv[c]
        diag_keep = g_diag[pl.ds(c, 1), :]
        entry = jnp.where(raw_f_in(c), raw_recv[c] + diag_keep * carried, carried)
        middle = jnp.where(odd, other, own) + jnp.where(odd, other_keep, own_keep) * entry
        onward = jnp.where(odd, own, other) + jnp.where(odd, own_keep, other_keep) * middle
        zf_send[c] = jnp.where(raw_f_pass(c), middle, onward)

        @pl.when(has_high)
        def _():
            zf(c).start()

        rf_send[c] = jnp.where(odd, entry, middle)

        @pl.when(from_last & ~via_f_skip(c))
        def _():
            rf(c).start()

        @pl.when(via_f_out(c))
        def _():
            via(zf_send, c).start()

        before_s[c, mine] = jnp.where(odd, middle, entry)

    def pass_forward(c):
        @pl.when(via_f_on(c))
        def _():
            via(zf_send, c).wait_recv()
            on_f(c).start()

    def pass_backward(c):
        @pl.when(via_b_on(c))
        def _():
            via(zb_send, c).wait_recv()
            on_b(c).start()

    def forward_step(c):
        @pl.when(to_last)
        def _():
            rf(c).wait_recv()

        before_h = before_s[c].astype(BF16)
        rise = rise_s[c]
        lifted = lift_s[c]
        y = rise * (mm(mixing, lifted) + mm(queries_open, before_h))
        grad = weight * (y - t_ref[:, lanes(c)].astype(F32))
        z = (grad * rise).astype(BF16)
        xb_send[c] = mm(queries_t, z)

        @pl.when(to_last & ~raw_b_out(c))
        def _():
            xb(c).start()

        @pl.when(raw_b_out(c))
        def _():
            raw(xb_send, c).start()

        out_ref[:, lanes(c)] = y.astype(BF16)
        y_s[c] = grad * y
        dq_s[...] += mm_nt(z, before_h)
        dmix_s[...] += mm_nt(z, lifted)
        dmixt_s[...] += mm_nt(lifted, z)
        dl_s[c] = mm(mixing_t, z)

    def sent_forward(c):
        @pl.when(to_next & ~raw_f_out(c))
        def _():
            xf(c).wait_send()

        @pl.when(raw_f_out(c))
        def _():
            raw(xf_send, c).wait_send()

        @pl.when(from_last & ~via_f_skip(c))
        def _():
            rf(c).wait_send()

        @pl.when(via_f_out(c))
        def _():
            via(zf_send, c).wait_send()

        @pl.when(via_f_on(c))
        def _():
            on_f(c).wait_send()

        @pl.when(has_high)
        def _():
            zf(c).wait_send()

    def sent_backward(c):
        @pl.when(to_last & ~raw_b_out(c))
        def _():
            xb(c).wait_send()

        @pl.when(raw_b_out(c))
        def _():
            raw(xb_send, c).wait_send()

        @pl.when(from_next & ~via_b_skip(c))
        def _():
            rb(c).wait_send()

        @pl.when(via_b_out(c))
        def _():
            via(zb_send, c).wait_send()

        @pl.when(via_b_on(c))
        def _():
            on_b(c).wait_send()

        @pl.when(has_low)
        def _():
            zb(c).wait_send()

    def carry_backward(c):
        @pl.when(has_high)
        def _():
            zb(c).wait_recv()

        @pl.when(from_last & ~raw_b_pass(c))
        def _():
            xb(c).wait_recv()

        @pl.when(raw_b_in(c))
        def _():
            raw(xb_send, c).wait_recv()

        own_keep = g_send[pl.ds(c, 1), :]
        other_keep = g_recv[pl.ds(c, 1), :]
        own = xb_send[c, mine]
        other = xb_recv[c]
        carried = zb_recv[c]
        diag_keep = g_diag[pl.ds(c, 1), :]
        entry = jnp.where(raw_b_in(c), raw_recv[c] + diag_keep * carried, carried)
        middle = jnp.where(odd, own, other) + jnp.where(odd, own_keep, other_keep) * entry
        onward = jnp.where(odd, other, own) + jnp.where(odd, other_keep, own_keep) * middle
        zb_send[c] = jnp.where(raw_b_pass(c), middle, onward)

        @pl.when(has_low)
        def _():
            zb(c).start()

        rb_send[c] = jnp.where(odd, middle, entry)

        @pl.when(from_next & ~via_b_skip(c))
        def _():
            rb(c).start()

        @pl.when(via_b_out(c))
        def _():
            via(zb_send, c).start()

        adjoint_s[c, mine] = jnp.where(odd, entry, middle)

        @pl.when(c == 0)
        def _():
            @pl.when(has_high)
            def _():
                single(wdown, whigh, 3, me).wait_recv()

            wdown[...] = whigh[...] + wpair[...]

            @pl.when(has_low)
            def _():
                single(wdown, whigh, 3, me - 2).start()

            om_s[...] = (length * n_seq * n_dp) / (wlow[...] + wpair[...] + whigh[...])

    def backward_step(c):
        @pl.when(to_next)
        def _():
            rb(c).wait_recv()

        over_mean = om_s[0:1, 0:1]
        e = spread(c)
        gain = rise_s[c, length - 1:length, :]
        adjoint = adjoint_s[c] * over_mean
        scaled = (adjoint * (gain * sigma)).astype(BF16)
        d_feature = inv_s[c] * (dl_s[c] * over_mean + mm(keys_tail, scaled))
        gf_ref[:, lanes(c)] = d_feature.astype(BF16)
        change = y_s[c] * over_mean - f_ref[:, lanes(c)].astype(F32) * d_feature
        change_hi, change_lo = split(change)
        rt_s[...] += mm_nt(e, change_hi) + mm_nt(e, change_lo)
        dk_s[...] += mm_nt(lift_s[c], scaled)
        after = xf_send[c] + g_send[pl.ds(c, 1), :] * before_s[c]
        end_hi, end_lo = split(adjoint * after)
        ex_s[...] += mm_nt(e, end_hi) + mm_nt(e, end_lo)
        sent_forward(c)

        @pl.when(c >= BEHIND)
        def _():
            sent_backward(c - BEHIND)

    def finish_scores():
        over_mean = om_s[0:1, 0:1]
        d_scores = (jnp.where(linked, dmix_s[...], 0.0) * (over_mean * sigma)).astype(BF16)
        d_scores_t = (jnp.where(linked_t, dmixt_s[...], 0.0) * (over_mean * sigma)).astype(BF16)
        gq_ref[...] = (mm(d_scores, keys) + (open_col * over_mean) * dq_s[...]).astype(BF16)
        gk_s[...] = mm(d_scores_t, queries)

    def step(i, _):
        @pl.when(i + lead < chunks)
        def _():
            fresh_and_send(i + lead, 0)

        @pl.when(i < chunks)
        def _():
            carry_forward(i)

        @pl.when((i >= lag_u) & (i < lag_u + chunks))
        def _():
            pass_forward(i - lag_u)

        @pl.when((i >= lag_y) & (i < lag_y + chunks))
        def _():
            forward_step(i - lag_y)

        @pl.when((i >= lag_z) & (i < lag_z + chunks))
        def _():
            carry_backward(i - lag_z)

        @pl.when((i >= lag_v) & (i < lag_v + chunks))
        def _():
            pass_backward(i - lag_v)

        @pl.when(i == jnp.maximum(chunks + lag_y, lag_z + 1))
        def _():
            finish_scores()

        @pl.when((i >= lag_b) & (i < lag_b + chunks))
        def _():
            backward_step(i - lag_b)

        return 0

    end = jnp.maximum(chunks + jnp.maximum(lag_b, jnp.maximum(lag_y + 1, lag_u)), lag_z + 2)
    lax.fori_loop(0, end, step, 0)

    gk_ref[...] = (gk_s[...] + tail_col * dk_s[...]).astype(BF16)
    rt_hi, rt_lo = split(rt_s[...])
    decay = mm(rt_hi, lower) + mm(rt_lo, lower) + jnp.sum(ex_s[...], axis=1, keepdims=True)
    gd_ref[...] = decay[:heads]

    def finish_step(c, _):
        sent_backward(c)
        return 0

    lax.fori_loop(max(chunks - BEHIND, 0), chunks, finish_step, 0)

    def finish_w(d, _):
        w_dp(d).wait_send()
        return 0

    lax.fori_loop(1, n_dp, finish_w, 0)
    single(g_send, g_recv, 0, partner).wait_send()

    @pl.when(has_diag)
    def _():
        single(g_send, g_diag, 4, diag).wait_send()
    single(wown, wside, 1, partner).wait_send()

    @pl.when(has_high)
    def _():
        single(wup, wlow, 2, me + 2).wait_send()

    @pl.when(has_low)
    def _():
        single(wdown, whigh, 3, me - 2).wait_send()


def store_kernel(*refs):
    count = len(refs) // 2
    sem = refs[-1]
    copies = [
        pltpu.make_async_copy(refs[i], refs[count + i], sem.at[i]) for i in range(count)
    ]
    for copy in copies:
        copy.start()
    for copy in copies:
        copy.wait()


def body(features, key_proj, query_proj, log_decay, doc_start, loss_weight, target):
    n_seq, n_dp = lax.axis_size("seq"), lax.axis_size("dp")
    length, width = features.shape[1:]
    state = key_proj.shape[2]
    heads = log_decay.shape[1]
    chunks = width // CHUNK
    vmem = pl.BlockSpec(memory_space=pltpu.VMEM)
    big = (chunks, length, CHUNK)
    small = (chunks, state, CHUNK)
    half = (chunks, state // 2, CHUNK)
    scratch = [
        pltpu.VMEM(small, F32), pltpu.VMEM(half, F32), pltpu.VMEM(half, F32),
        pltpu.VMEM(half, F32), pltpu.VMEM(half, F32),
        pltpu.VMEM(small, F32), pltpu.VMEM(half, F32), pltpu.VMEM(half, F32),
        pltpu.VMEM(half, F32), pltpu.VMEM(half, F32),
        pltpu.VMEM(small, F32), pltpu.VMEM(small, F32),
        pltpu.VMEM(half, F32), pltpu.VMEM(half, F32), pltpu.VMEM((chunks, CHUNK), F32),
        pltpu.VMEM((chunks, CHUNK), F32), pltpu.VMEM((chunks, CHUNK), F32),
        pltpu.VMEM(big, F32), pltpu.VMEM(big, F32), pltpu.VMEM(big, F32), pltpu.VMEM(big, F32),
        pltpu.VMEM(big, BF16),
        pltpu.VMEM((length, length), F32), pltpu.VMEM((length, length), F32),
        pltpu.VMEM((length, state), F32), pltpu.VMEM((length, state), F32),
        pltpu.VMEM((length, state), F32), pltpu.VMEM((128, length), F32), pltpu.VMEM((128, state), F32),
        pltpu.VMEM((8, 128), F32), pltpu.VMEM((n_dp - 1, 8, 128), F32),
    ]
    scratch += [pltpu.VMEM((8, 128), F32)] * 8
    scratch += [
        pltpu.VMEM((length, width), BF16), pltpu.VMEM((length, state), BF16),
        pltpu.VMEM((length, state), BF16), pltpu.VMEM((heads, length), F32),
        pltpu.VMEM((1, length), jnp.int32), pltpu.VMEM((1, length), F32),
        pltpu.VMEM((length, width), BF16), pltpu.SemaphoreType.DMA((7,)),
    ]
    scratch += [pltpu.SemaphoreType.DMA((chunks,))] * 17
    scratch += [pltpu.SemaphoreType.DMA((n_dp - 1,))] * 2
    scratch += [pltpu.SemaphoreType.DMA((5,))] * 2
    shapes = (
        ((length, width), BF16),
        ((length, width), BF16),
        ((length, state), BF16),
        ((length, state), BF16),
        ((heads, length), F32),
    )
    results = pl.pallas_call(
        functools.partial(kernel, n_seq, n_dp, heads),
        out_shape=tuple(pltpu.VMEM(*shape) for shape in shapes),
        in_specs=[pl.BlockSpec(memory_space=pltpu.HBM)] * 7,
        out_specs=(vmem,) * 5,
        scratch_shapes=scratch,
        compiler_params=pltpu.CompilerParams(
            collective_id=0, has_side_effects=True, vmem_limit_bytes=44 << 20
        ),
        name="mixing",
    )(
        *(
            pltpu.with_memory_space_constraint(x, pltpu.HBM)
            for x in (
                features[0], key_proj[0], query_proj[0], log_decay[0], doc_start, loss_weight,
                target[0],
            )
        )
    )
    stored = pl.pallas_call(
        store_kernel,
        out_shape=tuple(jax.ShapeDtypeStruct(*shape) for shape in shapes),
        in_specs=(vmem,) * 5,
        out_specs=(pl.BlockSpec(memory_space=pl.ANY),) * 5,
        scratch_shapes=[pltpu.SemaphoreType.DMA((5,))],
        name="store",
    )(*(pltpu.with_memory_space_constraint(r, pltpu.VMEM) for r in results))
    return tuple(r[None] for r in stored)


def solution(mesh):
    placed = (
        P("dp", "seq", None),
        P("dp", "seq", None),
        P("dp", "seq", None),
        P("dp", None, "seq"),
        P("dp", "seq"),
        P("dp", "seq"),
        P("dp", "seq", None),
    )
    return jax.shard_map(
        body,
        mesh=mesh,
        in_specs=placed,
        out_specs=(
            P("dp", "seq", None),
            P("dp", "seq", None),
            P("dp", "seq", None),
            P("dp", "seq", None),
            P("dp", None, "seq"),
        ),
        check_vma=False,
    )
```
